128 devices in a mesh: ti: 8 (over x_lo, z), tj: 16 (over y, x_hi, core).
Axes of the slice: x: 4 (x_hi: 2, x_lo: 2; x = x_hi * 2 + x_lo), y: 4, z: 4, core: 2. Of those that a mesh axis runs over, the one named last changes fastest.
Arguments:
- alignment_source: float32 [64, 256, 64], P('tj', 'ti'), may hold values from -6 to 6
- couple_source: float32 [256, 256, 128], P('ti', 'tj'), may hold values from -6 to 6
- tensor_operand_matrix: float32 [64, 64], replicated, may hold values from -0.75 to 0.75
- tensor_final_matrix: float32 [1024, 128], replicated, may hold values from -0.75 to 0.75
- mixing_content_matrix: float32 [64, 256], replicated, may hold values from -0.75 to 0.75
- mixing_switch_matrix: float32 [64, 256], replicated, may hold values from -0.75 to 0.75
- mixing_score_matrix: float32 [128, 8], replicated, may hold values from -48 to 48, as said below
- mixing_final_matrix: float32 [256, 64], replicated, may hold values from -0.375 to 0.375
- alignment_expand_matrix: float32 [64, 512], replicated, may hold values from -0.75 to 0.75
- alignment_shrink_matrix: float32 [256, 64], replicated, may hold values from -0.375 to 0.375
- couple_expand_matrix: float32 [128, 1024], replicated, may hold values from -0.5 to 0.5
- couple_shrink_matrix: float32 [512, 128], replicated, may hold values from -0.25 to 0.25
Outputs:
- alignment_result: float32 [64, 256, 64], P('tj', 'ti')
- couple_result: float32 [256, 256, 128], P('ti', 'tj')
The draws below stay inside these ranges and needn't reach their ends.
Inputs may be any that keep to these rules, and one draw needn't show every extreme that they name: `mixing_score_matrix`: each column is one head's logit projection.
All inputs are finite; a program needn't handle non-finite values.
Results may differ from the reference program's by a relative error of at most 0.00026.
Values sent between devices are 32-bit elements; how exact they have to be, the bound alone decides.
No kernel may reach another device: no remote copies, remote signals or barrier semaphores. Data moves between devices by JAX's collectives and lax.ppermute only.
A program may use at most 64 MiB of HBM per device.

```python
import jax
import jax.numpy as jnp
from jax import lax

ALIGN_FEATURES = 64
C_Z = 128
FACTOR_WIDTH = 32
MEAN_GROUPS = 8
GROUP_FEATURES = 32
ALIGN_INNER_SIZE = 256
PAIR_HID = 512
RESIDUE_COUNT = 256
SEQUENCE_COUNT = 64


def draw_mixing_score_matrix(key, part):
    base = jnp.clip(jax.random.normal(key, (C_Z, MEAN_GROUPS), jnp.float32), -4.0, 4.0) * 0.3
    return base


def levels(own_key, dims, shards, least, top_value):
    factor_of, own = 1.0, jax.random.fold_in(own_key, 6)
    for axis_at, blocks in shards:
        steps = jnp.exp(jax.random.uniform(jax.random.fold_in(own, axis_at), (blocks,), jnp.float32, least / len(shards), top_value / len(shards)))
        factor_of = factor_of * jnp.repeat(steps, dims[axis_at] // blocks).reshape([-1 if axis == axis_at else 1 for axis in range(len(dims))])
    return factor_of


def noise(rng, extent, spread, most, shards=(), held_as=jnp.bfloat16):
    array = spread * jax.random.normal(rng, extent, jnp.float32)
    if shards:
        array = array * levels(rng, extent, shards, -0.22, 0.18)
    return jnp.clip(array, -most, most).astype(held_as)


def setup_inputs(seed: int = 0) -> dict:
    keys = jax.random.split(jax.random.key(seed), 13)
    alignment_source = noise(keys[0], (SEQUENCE_COUNT, RESIDUE_COUNT, ALIGN_FEATURES), 1.0, 6.0, ((0, 16), (1, 8)), jnp.float32)
    couple_source = noise(keys[1], (RESIDUE_COUNT, RESIDUE_COUNT, C_Z), 1.0, 6.0, ((0, 8), (1, 16)), jnp.float32)
    tensor_operand_matrix = noise(keys[2], (ALIGN_FEATURES, 2 * FACTOR_WIDTH), ALIGN_FEATURES ** -0.5, 0.75, (), jnp.float32)
    tensor_final_matrix = noise(keys[3], (FACTOR_WIDTH * FACTOR_WIDTH, C_Z), (FACTOR_WIDTH * FACTOR_WIDTH // 16) ** -0.5, 0.75, (), jnp.float32)
    mixing_content_matrix = noise(keys[4], (ALIGN_FEATURES, MEAN_GROUPS * GROUP_FEATURES), ALIGN_FEATURES ** -0.5, 0.75, (), jnp.float32)
    mixing_switch_matrix = noise(keys[5], (ALIGN_FEATURES, MEAN_GROUPS * GROUP_FEATURES), ALIGN_FEATURES ** -0.5, 0.75, (), jnp.float32)
    mixing_score_matrix = draw_mixing_score_matrix(jax.random.fold_in(keys[12], 71), 0)
    mixing_final_matrix = noise(keys[7], (MEAN_GROUPS * GROUP_FEATURES, ALIGN_FEATURES), (MEAN_GROUPS * GROUP_FEATURES) ** -0.5, 0.375, (), jnp.float32)
    alignment_expand_matrix = noise(keys[8], (ALIGN_FEATURES, 2 * ALIGN_INNER_SIZE), ALIGN_FEATURES ** -0.5, 0.75, (), jnp.float32)
    alignment_shrink_matrix = noise(keys[9], (ALIGN_INNER_SIZE, ALIGN_FEATURES), ALIGN_INNER_SIZE ** -0.5, 0.375, (), jnp.float32)
    couple_expand_matrix = noise(keys[10], (C_Z, 2 * PAIR_HID), C_Z ** -0.5, 0.5, (), jnp.float32)
    couple_shrink_matrix = noise(keys[11], (PAIR_HID, C_Z), PAIR_HID ** -0.5, 0.25, (), jnp.float32)
    return {"alignment_source": alignment_source, "couple_source": couple_source, "tensor_operand_matrix": tensor_operand_matrix, "tensor_final_matrix": tensor_final_matrix, "mixing_content_matrix": mixing_content_matrix, "mixing_switch_matrix": mixing_switch_matrix, "mixing_score_matrix": mixing_score_matrix, "mixing_final_matrix": mixing_final_matrix, "alignment_expand_matrix": alignment_expand_matrix, "alignment_shrink_matrix": alignment_shrink_matrix, "couple_expand_matrix": couple_expand_matrix, "couple_shrink_matrix": couple_shrink_matrix}


exact_arithmetic = lax.Precision.HIGHEST
epsilon = 1e-05

def feature_standardize(inputs):
    mean_val = lax.optimization_barrier(jnp.mean(inputs, axis=-1, keepdims=True))
    centred = inputs - mean_val
    variance = lax.optimization_barrier(jnp.mean(centred * centred, axis=-1, keepdims=True))
    return centred * lax.rsqrt(variance + epsilon)

def feedforward_block(inputs, gate_up, down):
    hidden = jnp.einsum('...c,cd->...d', inputs, gate_up, precision=exact_arithmetic)
    half_width = down.shape[0]
    activated = jax.nn.silu(hidden[..., :half_width]) * hidden[..., half_width:]
    return jnp.einsum('...c,cd->...d', activated, down, precision=exact_arithmetic)

def reference(alignment_source, couple_source, tensor_operand_matrix, tensor_final_matrix, mixing_content_matrix, mixing_switch_matrix, mixing_score_matrix, mixing_final_matrix, alignment_expand_matrix, alignment_shrink_matrix, couple_expand_matrix, couple_shrink_matrix):
    sequence_count_all = alignment_source.shape[0]
    residue_count_all = alignment_source.shape[1]
    alignment_standardized = feature_standardize(alignment_source)
    tensor_operands = jnp.einsum('zji,in->zjn', alignment_standardized, tensor_operand_matrix, precision=exact_arithmetic)
    left_proj = tensor_operands[..., :FACTOR_WIDTH]
    right_proj = tensor_operands[..., FACTOR_WIDTH:]
    block_size = min(32, residue_count_all)
    block_count = residue_count_all // block_size
    left_blocks = left_proj.reshape(sequence_count_all, block_count, block_size, FACTOR_WIDTH).transpose(1, 0, 2, 3)
    pair_blocks = couple_source.reshape(block_count, block_size, residue_count_all, C_Z)

    def pair_block(inputs_pair):
        left_block, pair_rows = inputs_pair
        outer_prod = jnp.einsum('sia,sjb->ijab', left_block, right_proj, precision=exact_arithmetic) / sequence_count_all
        flattened = outer_prod.reshape(-1, FACTOR_WIDTH * FACTOR_WIDTH)
        update = jnp.dot(flattened, tensor_final_matrix, precision=exact_arithmetic, preferred_element_type=jnp.float32)
        pair_mid = pair_rows + update.reshape(pair_rows.shape)
        pair_normed = feature_standardize(pair_mid)
        logits = jnp.einsum('ijc,ch->hij', pair_normed, mixing_score_matrix, precision=exact_arithmetic)
        pair_next = pair_mid + feedforward_block(pair_normed, couple_expand_matrix, couple_shrink_matrix)
        return (pair_next, logits)
    pair_next, logit_blocks = lax.map(pair_block, (left_blocks, pair_blocks))
    couple_result = pair_next.reshape(residue_count_all, residue_count_all, C_Z)
    logits = logit_blocks.transpose(1, 0, 2, 3).reshape(MEAN_GROUPS, residue_count_all, residue_count_all)
    row_max = lax.optimization_barrier(jnp.max(logits, axis=2, keepdims=True))
    exp_terms = jnp.exp(logits - row_max)
    weights = exp_terms / lax.optimization_barrier(jnp.sum(exp_terms, axis=2, keepdims=True))
    content_sequences = jnp.einsum('jzb,bq->jzq', alignment_standardized, mixing_content_matrix, precision=exact_arithmetic).reshape(sequence_count_all, residue_count_all, MEAN_GROUPS, GROUP_FEATURES)
    sigmoid_switch = jax.nn.sigmoid(jnp.einsum('zji,in->zjn', alignment_standardized, mixing_switch_matrix, precision=exact_arithmetic))
    group_mixed = jnp.einsum('hij,sjhc->sihc', weights, content_sequences, precision=exact_arithmetic).reshape(sequence_count_all, residue_count_all, MEAN_GROUPS * GROUP_FEATURES)
    alignment_between = alignment_source + jnp.einsum('xvr,rq->xvq', sigmoid_switch * group_mixed, mixing_final_matrix, precision=exact_arithmetic)
    alignment_result = alignment_between + feedforward_block(feature_standardize(alignment_between), alignment_expand_matrix, alignment_shrink_matrix)
    return (alignment_result, couple_result)
```

```python
import functools

import jax
import jax.numpy as jnp
from jax import lax
from jax.experimental import pallas as pl
from jax.experimental.pallas import tpu as pltpu
from jax.sharding import PartitionSpec as P

F32 = jnp.float32
BF16 = jnp.bfloat16
EPS = 1e-05
TI = 8
TJ = 16
ROWS = 4
TOK = 32
COLS = 16
NN = (((1,), (0,)), ((), ()))
NT = (((1,), (1,)), ((), ()))


def dot(a, b, dims=NN):
    return lax.dot_general(a, b, dims, preferred_element_type=F32)


def split(x):
    hi = x.astype(BF16)
    return hi, (x - hi.astype(F32)).astype(BF16)


def dot3(a, b, dims=NN):
    (ah, al), (bh, bl) = a, b
    return dot(ah, bh, dims) + dot(ah, bl, dims) + dot(al, bh, dims)


def iota(shape, dim):
    return lax.broadcasted_iota(jnp.int32, shape, dim)


def normed(x):
    centred = x - jnp.mean(x, axis=-1, keepdims=True)
    var = jnp.mean(centred * centred, axis=-1, keepdims=True)
    return centred * lax.rsqrt(var + EPS)


def spread_heads(w):
    n, l = iota((256, 1024), 0), iota((256, 1024), 1)
    place = (n == (l // 128) * 32 + l % 32).astype(BF16)
    wide = dot(w, place)
    tall = jnp.concatenate([wide] * 4, axis=0)
    keep = iota((256, 1024), 0) // 64 == (iota((256, 1024), 1) // 32) % 4
    return jnp.where(keep, tall, 0.0)


def first_kernel(x_ref, send_ref):
    x = normed(x_ref[...])
    low = jnp.concatenate([x[0], x[1]], axis=1)
    high = jnp.concatenate([x[2], x[3]], axis=1)
    for d in range(TI):
        send_ref[d, :TOK, :] = low
        send_ref[d, TOK:, :] = high


def left_kernel(own_ref, w_ref, left_ref, wr_hi_ref, wr_lo_ref):
    x = jnp.concatenate([own_ref[0, :TOK, :], own_ref[0, TOK:, :]], axis=1)
    xs = split(jnp.concatenate([x] * 4, axis=0))
    ws = split(w_ref[...])
    pick = (iota((128, 64), 0) // 4 == iota((128, 64), 1)).astype(BF16)
    tile_k = (iota((64, 256), 0) == iota((64, 256), 1) % 64).astype(BF16)
    keep = iota((128, 256), 0) % 4 == iota((128, 256), 1) // 64
    wl = []
    for part in ws:
        rows = dot(pick, part, NT).astype(BF16)
        wl.append(jnp.where(keep, dot(rows, tile_k), 0.0).astype(BF16))
    prod = dot3(tuple(wl), xs, NT) * (1.0 / 64.0)
    group = iota((16, 128), 1) // 32
    for half in range(2):
        out = jnp.zeros((16, 128), F32)
        for q in range(4):
            at = half * 64 + q * 16
            out = jnp.where(group == q, prod[at : at + 16], out)
        left_ref[half * 16 : half * 16 + 16, :] = out
    tile_b = (iota((64, 128), 0) == 32 + iota((64, 128), 1) % 32).astype(BF16)
    keep_r = iota((256, 128), 0) // 64 == iota((256, 128), 1) // 32
    for part, ref in zip(ws, (wr_hi_ref, wr_lo_ref)):
        tall = jnp.concatenate([dot(part, tile_b)] * 4, axis=0)
        ref[...] = jnp.where(keep_r, tall, 0.0).astype(BF16)


def all_tokens(recv_ref):
    return (
        recv_ref[:, :TOK, :].reshape(TI * TOK, 128),
        recv_ref[:, TOK:, :].reshape(TI * TOK, 128),
    )


def right_kernel(recv_ref, left_ref, wr_hi_ref, wr_lo_ref, send_ref):
    low, high = all_tokens(recv_ref)
    wh, wl = wr_hi_ref[...], wr_lo_ref[...]
    right = dot3(split(low), (wh[:128], wl[:128])) + dot3(split(high), (wh[128:], wl[128:]))
    left = left_ref[...]
    for d in range(TJ):
        send_ref[d, :32, :] = left
        send_ref[d, 32:, :] = right[d * COLS : (d + 1) * COLS]


def values_kernel(recv_ref, wv_ref, t_ref, score_ref, v_ref, t_out_ref, score_out_ref):
    low, high = all_tokens(recv_ref)
    wv = [spread_heads(part).astype(BF16) for part in split(wv_ref[...])]
    xs = split(jnp.concatenate([low, high], axis=1))
    for h in range(8):
        cols = slice(h * 128, (h + 1) * 128)
        vh, vl = split(dot3(xs, (wv[0][:, cols], wv[1][:, cols])))
        for d in range(TJ):
            at = (d * 8 + h) * COLS
            v_ref[at : at + COLS, :128] = vh[d * COLS : (d + 1) * COLS]
            v_ref[at : at + COLS, 128:] = vl[d * COLS : (d + 1) * COLS]
    th, tl = split(t_ref[...])
    t_out_ref[:, :128] = th
    t_out_ref[:, 128:] = tl
    score = score_ref[...]
    tall = jnp.concatenate([jnp.broadcast_to(score[h : h + 1], (16, 128)) for h in range(8)], axis=0)
    sh, sl = split(tall.T)
    score_out_ref[:, :128] = sh
    score_out_ref[:, 128:] = sl


def pair_kernel(recv_ref, pair_ref, t_ref, score_ref, mid_ref, send_ref, f_hi, f_lo):
    rows = [
        jnp.concatenate([recv_ref[:, r, :], recv_ref[:, 16 + r, :]], axis=1) for r in range(16)
    ]
    left = jnp.concatenate(rows, axis=0).T
    lh, ll = split(left)
    left3 = jnp.concatenate([lh, lh, ll], axis=1)
    group = iota((16, 128), 1) // 32
    zero = jnp.zeros((16, 128), BF16)
    for pair in range(COLS // 2):
        blocks = []
        for j in (2 * pair, 2 * pair + 1):
            right = recv_ref[:, 32 + j, :]
            turned = [split(pltpu.roll(right, 32 * d, 1) if d else right) for d in range(4)]
            parts = []
            for which in range(2):
                tiles = [
                    jnp.where(group == a, turned[(a - s) % 4][which], zero)
                    for a in range(4)
                    for s in range(4)
                ]
                parts.append(jnp.concatenate(tiles, axis=0))
            blocks.append(jnp.concatenate([parts[0], parts[1], parts[0]], axis=0))
        outer = dot(left3, jnp.concatenate(blocks, axis=1))
        oh, ol = split(outer)
        for q in range(2):
            at = (2 * pair + q) * TOK
            for g in range(8):
                take = (slice(g * 32, g * 32 + 32), slice(q * 128, q * 128 + 128))
                f_hi[at : at + TOK, g * 128 : g * 128 + 128] = oh[take]
                f_lo[at : at + TOK, g * 128 : g * 128 + 128] = ol[take]
    wide = dot(f_hi[...], t_ref[...])
    update = wide[:, :128] + wide[:, 128:] + dot(f_lo[...], t_ref[:, :128])
    normal = []
    for j in range(COLS):
        mid = pair_ref[:, j, :] + update[j * TOK : (j + 1) * TOK]
        mid_ref[j] = mid
        normal.append(normed(mid))
    nh, nl = split(jnp.concatenate(normal, axis=0))
    wide = dot(nh, score_ref[...])
    logits = wide[:, :128] + wide[:, 128:] + dot(nl, score_ref[:, :128])
    column = iota((TOK, 128), 1) % 16
    tile = jnp.zeros((TOK, 128), F32)
    for j in range(COLS):
        tile = jnp.where(column == j, logits[j * TOK : (j + 1) * TOK], tile)
    for d in range(TJ):
        send_ref[d] = tile


def pair_transition_kernel(mid_ref, expand_ref, shrink_ref, out_ref):
    eh, el = split(expand_ref[...])
    expand3 = jnp.concatenate([eh, eh, el], axis=0)
    sh, sl = split(shrink_ref[...])
    shrink2 = jnp.concatenate([sh, sl], axis=1)
    step = 4
    for at in range(0, COLS, step):
        mid = mid_ref[at : at + step].reshape(step * TOK, 128)
        nh, nl = split(normed(mid))
        hidden = dot(jnp.concatenate([nh, nl, nh], axis=1), expand3)
        gate = hidden[:, :512]
        act = gate / (1.0 + jnp.exp(-gate)) * hidden[:, 512:]
        ah, al = split(act)
        wide = dot(ah, shrink2)
        out = mid + wide[:, :128] + wide[:, 128:] + dot(al, sh)
        for j in range(step):
            out_ref[:, at + j, :] = out[j * TOK : (j + 1) * TOK]


def gates_kernel(own_ref, wg_ref, wf_ref, gate_ref, wf_hi_ref, wf_lo_ref):
    x = jnp.concatenate([own_ref[0, :TOK, :], own_ref[0, TOK:, :]], axis=1)
    wg = tuple(spread_heads(part).astype(BF16) for part in split(wg_ref[...]))
    logit = dot3(split(x), wg)
    gate_ref[...] = 1.0 / (1.0 + jnp.exp(-logit))
    for part, ref in zip(split(wf_ref[...]), (wf_hi_ref, wf_lo_ref)):
        ref[...] = spread_heads(part).T.astype(BF16)


def group_all(x, op):
    lane = iota(x.shape, 1)
    for d in (8, 4, 2, 1):
        other = jnp.where((lane & d) == 0, pltpu.roll(x, 128 - d, 1), pltpu.roll(x, d, 1))
        x = op(x, other)
    return x


def last_kernel(
    recv_ref, v_ref, gate_ref, wf_hi_ref, wf_lo_ref, x_ref, expand_ref, shrink_ref, out_ref, w_hi, w_lo
):
    top = recv_ref[0]
    for d in range(1, TJ):
        top = jnp.maximum(top, recv_ref[d])
    top = group_all(top, jnp.maximum)
    terms = [jnp.exp(recv_ref[d] - top) for d in range(TJ)]
    total = terms[0]
    for d in range(1, TJ):
        total = total + terms[d]
    inv = 1.0 / group_all(total, jnp.add)
    head = iota((TOK, 128), 1) // 16
    zero = jnp.zeros((TOK, 128), BF16)
    for d in range(TJ):
        wh, wl = split(terms[d] * inv)
        for h in range(8):
            w_hi[h * TOK : (h + 1) * TOK, d * 128 : d * 128 + 128] = jnp.where(head == h, wh, zero)
            w_lo[h * TOK : (h + 1) * TOK, d * 128 : d * 128 + 128] = jnp.where(head == h, wl, zero)
    wide = dot(w_hi[...], v_ref[...])
    mixed = wide[:, :128] + wide[:, 128:] + dot(w_lo[...], v_ref[:, :128])
    gated = gate_ref[...] * jnp.concatenate([mixed[h * TOK : (h + 1) * TOK] for h in range(8)], axis=1)
    update = dot3(split(gated), (wf_hi_ref[...], wf_lo_ref[...]))
    mid = jnp.concatenate(
        [x_ref[s] + update[:, s * 64 : (s + 1) * 64] for s in range(ROWS)], axis=0
    )
    hidden = dot3(split(normed(mid)), split(expand_ref[...]))
    gate = hidden[:, :256]
    act = gate / (1.0 + jnp.exp(-gate)) * hidden[:, 256:]
    out = mid + dot3(split(act), split(shrink_ref[...]), NT)
    out_ref[...] = out.reshape(ROWS, TOK, 64)


def call(kernel, outs, *args, specs=None, scratch=(), flops=0):
    vmem = pl.BlockSpec(memory_space=pltpu.VMEM)
    in_specs = [vmem] * len(args) if specs is None else [s or vmem for s in specs]
    single = not isinstance(outs, (list, tuple))
    outs = [outs] if single else list(outs)
    moved = sum(a.size * a.dtype.itemsize for a in args) + sum(
        o.size * o.dtype.itemsize for o in outs
    )
    res = pl.pallas_call(
        kernel,
        out_shape=outs,
        in_specs=in_specs,
        out_specs=[vmem] * len(outs),
        scratch_shapes=list(scratch),
        compiler_params=pltpu.CompilerParams(vmem_limit_bytes=24 << 20),
        cost_estimate=pl.CostEstimate(flops=flops, bytes_accessed=moved, transcendentals=0),
    )(*args)
    return res[0] if single else res


def shape(dims, dtype=F32):
    return jax.ShapeDtypeStruct(dims, dtype)


def shards(
    alignment_source,
    couple_source,
    tensor_operand_matrix,
    tensor_final_matrix,
    mixing_content_matrix,
    mixing_switch_matrix,
    mixing_score_matrix,
    mixing_final_matrix,
    alignment_expand_matrix,
    alignment_shrink_matrix,
    couple_expand_matrix,
    couple_shrink_matrix,
):
    exchange = functools.partial(lax.all_to_all, split_axis=0, concat_axis=0, tiled=True)
    own = call(first_kernel, shape((TI, 64, 128)), alignment_source)
    tokens = exchange(own, "ti")
    left, wr_hi, wr_lo = call(
        left_kernel,
        [shape((32, 128)), shape((256, 128), BF16), shape((256, 128), BF16)],
        own,
        tensor_operand_matrix,
        flops=100_000_000,
    )
    factors = call(right_kernel, shape((TJ, 48, 128)), tokens, left, wr_hi, wr_lo)
    factors = exchange(factors, "tj")
    values, final2, score2 = call(
        values_kernel,
        [shape((2048, 256), BF16), shape((1024, 256), BF16), shape((128, 256), BF16)],
        tokens,
        mixing_content_matrix,
        tensor_final_matrix,
        mixing_score_matrix.T,
        flops=1_000_000_000,
    )
    mid, logits = call(
        pair_kernel,
        [shape((COLS, TOK, 128)), shape((TJ, TOK, 128))],
        factors,
        couple_source,
        final2,
        score2,
        scratch=[pltpu.VMEM((512, 1024), BF16), pltpu.VMEM((512, 1024), BF16)],
        flops=2_000_000_000,
    )
    logits = exchange(logits, "tj")
    couple_result = call(
        pair_transition_kernel,
        shape((TOK, COLS, 128)),
        mid,
        couple_expand_matrix,
        couple_shrink_matrix,
        flops=1_000_000_000,
    )
    gates, wf_hi, wf_lo = call(
        gates_kernel,
        [shape((32, 1024)), shape((1024, 256), BF16), shape((1024, 256), BF16)],
        own,
        mixing_switch_matrix,
        mixing_final_matrix.T,
        flops=500_000_000,
    )
    alignment_result = call(
        last_kernel,
        shape((ROWS, TOK, 64)),
        logits,
        values,
        gates,
        wf_hi,
        wf_lo,
        alignment_source,
        alignment_expand_matrix,
        alignment_shrink_matrix.T,
        scratch=[pltpu.VMEM((256, 2048), BF16), pltpu.VMEM((256, 2048), BF16)],
        flops=500_000_000,
    )
    return (alignment_result, couple_result)


def solution(mesh):
    rows, pairs = P("tj", "ti", None), P("ti", "tj", None)
    return jax.shard_map(
        shards,
        mesh=mesh,
        in_specs=(rows, pairs) + (P(),) * 10,
        out_specs=(rows, pairs),
        check_vma=False,
    )
```

```python
import functools

import jax
import jax.numpy as jnp
from jax import lax
from jax.experimental import pallas as pl
from jax.experimental.pallas import tpu as pltpu
from jax.sharding import PartitionSpec as P

F32 = jnp.float32
BF16 = jnp.bfloat16
EPS = 1e-05
TI = 8
TJ = 16
ROWS = 4
TOK = 32
COLS = 16
NN = (((1,), (0,)), ((), ()))
NT = (((1,), (1,)), ((), ()))


def dot(a, b, dims=NN):
    return lax.dot_general(a, b, dims, preferred_element_type=F32)


def split(x):
    hi = x.astype(BF16)
    return hi, (x - hi.astype(F32)).astype(BF16)


def dot3(a, b, dims=NN):
    (ah, al), (bh, bl) = a, b
    return dot(ah, bh, dims) + dot(ah, bl, dims) + dot(al, bh, dims)


def iota(shape, dim):
    return lax.broadcasted_iota(jnp.int32, shape, dim)


def normed(x):
    centred = x - jnp.mean(x, axis=-1, keepdims=True)
    var = jnp.mean(centred * centred, axis=-1, keepdims=True)
    return centred * lax.rsqrt(var + EPS)


def head_tiles(w):
    group = iota((64, 128), 1) // 32
    tiles = []
    for half in range(2):
        part = w[:, half * 128 : half * 128 + 128]
        turned = [pltpu.roll(part, 32 * d, 1) if d else part for d in range(4)]
        for q in range(4):
            tile = turned[(3 - q) % 4]
            for s in range(3):
                tile = jnp.where(group == s, turned[(s - q) % 4], tile)
            tiles.append(tile)
    return tiles


def head_weights(w):
    group = iota((64, 128), 1) // 32
    zero = jnp.zeros((64, 128), BF16)
    out = []
    for tile in head_tiles(w):
        out.append(
            tuple(
                jnp.concatenate([jnp.where(group == s, part, zero) for s in range(ROWS)], axis=0)
                for part in split(tile)
            )
        )
    return out


def first_kernel(x_ref, send_ref, own_ref):
    x = normed(x_ref[...])
    low = jnp.concatenate([x[0], x[1]], axis=1)
    high = jnp.concatenate([x[2], x[3]], axis=1)
    own_ref[:, :128] = low
    own_ref[:, 128:] = high
    for d in range(TI):
        send_ref[d, :TOK, :] = low
        send_ref[d, TOK:, :] = high


def prepare_kernel(
    own_ref, w_ref, t_ref, score_ref, wg_ref, wf_ref,
    left_ref, wr_hi_ref, wr_lo_ref, t_out_ref, score_out_ref, gate_ref, wf_hi_ref, wf_lo_ref,
):
    x = own_ref[...]
    one = split(x)
    xs = tuple(jnp.concatenate([part] * 4, axis=0) for part in one)
    ws = split(w_ref[...])
    pick = (iota((128, 64), 0) // 4 == iota((128, 64), 1)).astype(BF16)
    tile_k = (iota((64, 256), 0) == iota((64, 256), 1) % 64).astype(BF16)
    keep = iota((128, 256), 0) % 4 == iota((128, 256), 1) // 64
    wl = []
    for part in ws:
        rows = dot(pick, part, NT).astype(BF16)
        wl.append(jnp.where(keep, dot(rows, tile_k), 0.0).astype(BF16))
    prod = dot3(tuple(wl), xs, NT) * (1.0 / 64.0)
    group = iota((16, 128), 1) // 32
    for half in range(2):
        out = jnp.zeros((16, 128), F32)
        for q in range(4):
            at = half * 64 + q * 16
            out = jnp.where(group == q, prod[at : at + 16], out)
        left_ref[half * 16 : half * 16 + 16, :] = out
    tile_b = (iota((64, 128), 0) == 32 + iota((64, 128), 1) % 32).astype(BF16)
    keep_r = iota((256, 128), 0) // 64 == iota((256, 128), 1) // 32
    for part, ref in zip(ws, (wr_hi_ref, wr_lo_ref)):
        tall = jnp.concatenate([dot(part, tile_b)] * 4, axis=0)
        ref[...] = jnp.where(keep_r, tall, 0.0).astype(BF16)
    th, tl = split(t_ref[...])
    t_out_ref[:, :128] = th
    t_out_ref[:, 128:] = tl
    score = score_ref[...]
    tall = jnp.concatenate([jnp.broadcast_to(score[h : h + 1], (16, 128)) for h in range(8)], axis=0)
    sh, sl = split(tall.T)
    score_out_ref[:, :128] = sh
    score_out_ref[:, 128:] = sl
    for h, wg in enumerate(head_weights(wg_ref[...])):
        gate_ref[:, h * 128 : h * 128 + 128] = 1.0 / (1.0 + jnp.exp(-dot3(one, wg)))
    row = iota((32, 256), 1) // 64
    zero = jnp.zeros((32, 256), BF16)
    for part, ref in zip(split(wf_ref[...].T), (wf_hi_ref, wf_lo_ref)):
        wide = dot(part, tile_k).astype(BF16)
        for h in range(8):
            for s in range(ROWS):
                at = h * 128 + s * 32
                ref[at : at + 32, :] = jnp.where(row == s, wide[h * 32 : h * 32 + 32], zero)


def all_tokens(recv_ref):
    return (
        recv_ref[:, :TOK, :].reshape(TI * TOK, 128),
        recv_ref[:, TOK:, :].reshape(TI * TOK, 128),
    )


def right_kernel(recv_ref, left_ref, wr_hi_ref, wr_lo_ref, send_ref):
    low, high = all_tokens(recv_ref)
    wh, wl = wr_hi_ref[...], wr_lo_ref[...]
    right = dot3(split(low), (wh[:128], wl[:128])) + dot3(split(high), (wh[128:], wl[128:]))
    left = left_ref[...]
    for d in range(TJ):
        send_ref[d, :32, :] = left
        send_ref[d, 32:, :] = right[d * COLS : (d + 1) * COLS]


def values_kernel(recv_ref, wv_ref, v_ref):
    low, high = all_tokens(recv_ref)
    xs = split(jnp.concatenate([low, high], axis=1))
    for h, wv in enumerate(head_weights(wv_ref[...])):
        vh, vl = split(dot3(xs, wv))
        for d in range(TJ):
            at = (d * 8 + h) * COLS
            v_ref[at : at + COLS, :128] = vh[d * COLS : (d + 1) * COLS]
            v_ref[at : at + COLS, 128:] = vl[d * COLS : (d + 1) * COLS]


def pair_kernel(recv_ref, pair_ref, t_ref, score_ref, mid_ref, send_ref, f_hi, f_lo):
    rows = [
        jnp.concatenate([recv_ref[:, r, :], recv_ref[:, 16 + r, :]], axis=1) for r in range(16)
    ]
    left = jnp.concatenate(rows, axis=0).T
    lh, ll = split(left)
    left3 = jnp.concatenate([lh, lh, ll], axis=1)
    group = iota((16, 128), 1) // 32
    zero = jnp.zeros((16, 128), BF16)
    for pair in range(COLS // 2):
        blocks = []
        for j in (2 * pair, 2 * pair + 1):
            right = recv_ref[:, 32 + j, :]
            turned = [split(pltpu.roll(right, 32 * d, 1) if d else right) for d in range(4)]
            parts = []
            for which in range(2):
                tiles = [
                    jnp.where(group == a, turned[(a - s) % 4][which], zero)
                    for a in range(4)
                    for s in range(4)
                ]
                parts.append(jnp.concatenate(tiles, axis=0))
            blocks.append(jnp.concatenate([parts[0], parts[1], parts[0]], axis=0))
        outer = dot(left3, jnp.concatenate(blocks, axis=1))
        oh, ol = split(outer)
        for q in range(2):
            at = (2 * pair + q) * TOK
            for g in range(8):
                take = (slice(g * 32, g * 32 + 32), slice(q * 128, q * 128 + 128))
                f_hi[at : at + TOK, g * 128 : g * 128 + 128] = oh[take]
                f_lo[at : at + TOK, g * 128 : g * 128 + 128] = ol[take]
    wide = dot(f_hi[...], t_ref[...])
    update = wide[:, :128] + wide[:, 128:] + dot(f_lo[...], t_ref[:, :128])
    normal = []
    for j in range(COLS):
        mid = pair_ref[:, j, :] + update[j * TOK : (j + 1) * TOK]
        mid_ref[j] = mid
        normal.append(normed(mid))
    nh, nl = split(jnp.concatenate(normal, axis=0))
    wide = dot(nh, score_ref[...])
    logits = wide[:, :128] + wide[:, 128:] + dot(nl, score_ref[:, :128])
    column = iota((TOK, 128), 1) % 16
    tile = jnp.zeros((TOK, 128), F32)
    for j in range(COLS):
        tile = jnp.where(column == j, logits[j * TOK : (j + 1) * TOK], tile)
    for d in range(TJ):
        send_ref[d] = tile


def pair_transition_kernel(mid_ref, expand_ref, shrink_ref, out_ref):
    eh, el = split(expand_ref[...])
    expand3 = jnp.concatenate([eh, eh, el], axis=0)
    sh, sl = split(shrink_ref[...])
    shrink2 = jnp.concatenate([sh, sl], axis=1)
    step = 4
    for at in range(0, COLS, step):
        mid = mid_ref[at : at + step].reshape(step * TOK, 128)
        nh, nl = split(normed(mid))
        hidden = dot(jnp.concatenate([nh, nl, nh], axis=1), expand3)
        gate = hidden[:, :512]
        act = gate / (1.0 + jnp.exp(-gate)) * hidden[:, 512:]
        ah, al = split(act)
        wide = dot(ah, shrink2)
        out = mid + wide[:, :128] + wide[:, 128:] + dot(al, sh)
        for j in range(step):
            out_ref[:, at + j, :] = out[j * TOK : (j + 1) * TOK]


def group_all(x, op):
    lane = iota(x.shape, 1)
    for d in (8, 4, 2, 1):
        other = jnp.where((lane & d) == 0, pltpu.roll(x, 128 - d, 1), pltpu.roll(x, d, 1))
        x = op(x, other)
    return x


def last_kernel(
    recv_ref, v_ref, gate_ref, wf_hi_ref, wf_lo_ref, x_ref, expand_ref, shrink_ref, out_ref, w_hi, w_lo
):
    top = recv_ref[0]
    for d in range(1, TJ):
        top = jnp.maximum(top, recv_ref[d])
    top = group_all(top, jnp.maximum)
    terms = [jnp.exp(recv_ref[d] - top) for d in range(TJ)]
    total = terms[0]
    for d in range(1, TJ):
        total = total + terms[d]
    inv = 1.0 / group_all(total, jnp.add)
    head = iota((TOK, 128), 1) // 16
    zero = jnp.zeros((TOK, 128), BF16)
    for d in range(TJ):
        wh, wl = split(terms[d])
        for h in range(8):
            w_hi[h * TOK : (h + 1) * TOK, d * 128 : d * 128 + 128] = jnp.where(head == h, wh, zero)
            w_lo[h * TOK : (h + 1) * TOK, d * 128 : d * 128 + 128] = jnp.where(head == h, wl, zero)
    wide = dot(w_hi[...], v_ref[...])
    mixed = wide[:, :128] + wide[:, 128:] + dot(w_lo[...], v_ref[:, :128])
    gated = jnp.concatenate(
        [
            mixed[h * TOK : (h + 1) * TOK]
            * (gate_ref[:, h * 128 : h * 128 + 128] * inv[:, h * 16 : h * 16 + 1])
            for h in range(8)
        ],
        axis=1,
    )
    update = dot3(split(gated), (wf_hi_ref[...], wf_lo_ref[...]))
    mid = jnp.concatenate(
        [x_ref[s] + update[:, s * 64 : (s + 1) * 64] for s in range(ROWS)], axis=0
    )
    hidden = dot3(split(normed(mid)), split(expand_ref[...]))
    gate = hidden[:, :256]
    act = gate / (1.0 + jnp.exp(-gate)) * hidden[:, 256:]
    out = mid + dot3(split(act), split(shrink_ref[...]), NT)
    out_ref[...] = out.reshape(ROWS, TOK, 64)


def call(kernel, outs, *args, specs=None, scratch=(), flops=0):
    vmem = pl.BlockSpec(memory_space=pltpu.VMEM)
    in_specs = [vmem] * len(args) if specs is None else [s or vmem for s in specs]
    single = not isinstance(outs, (list, tuple))
    outs = [outs] if single else list(outs)
    moved = sum(a.size * a.dtype.itemsize for a in args) + sum(
        o.size * o.dtype.itemsize for o in outs
    )
    res = pl.pallas_call(
        kernel,
        out_shape=outs,
        in_specs=in_specs,
        out_specs=[vmem] * len(outs),
        scratch_shapes=list(scratch),
        compiler_params=pltpu.CompilerParams(vmem_limit_bytes=24 << 20),
        cost_estimate=pl.CostEstimate(flops=flops, bytes_accessed=moved, transcendentals=0),
    )(*args)
    return res[0] if single else res


def shape(dims, dtype=F32):
    return jax.ShapeDtypeStruct(dims, dtype)


def shards(
    alignment_source,
    couple_source,
    tensor_operand_matrix,
    tensor_final_matrix,
    mixing_content_matrix,
    mixing_switch_matrix,
    mixing_score_matrix,
    mixing_final_matrix,
    alignment_expand_matrix,
    alignment_shrink_matrix,
    couple_expand_matrix,
    couple_shrink_matrix,
):
    exchange = functools.partial(lax.all_to_all, split_axis=0, concat_axis=0, tiled=True)
    send, own = call(first_kernel, [shape((TI, 64, 128)), shape((TOK, 256))], alignment_source)
    tokens = exchange(send, "ti")
    prepared = call(
        prepare_kernel,
        [shape((32, 128)), shape((256, 128), BF16), shape((256, 128), BF16)]
        + [shape((1024, 256), BF16), shape((128, 256), BF16), shape((32, 1024))]
        + [shape((1024, 256), BF16), shape((1024, 256), BF16)],
        own,
        tensor_operand_matrix,
        tensor_final_matrix,
        mixing_score_matrix.T,
        mixing_switch_matrix,
        mixing_final_matrix.T,
        flops=500_000_000,
    )
    left, wr_hi, wr_lo, final2, score2, gates, wf_hi, wf_lo = prepared
    factors = call(right_kernel, shape((TJ, 48, 128)), tokens, left, wr_hi, wr_lo)
    factors = exchange(factors, "tj")
    mid, logits = call(
        pair_kernel,
        [shape((COLS, TOK, 128)), shape((TJ, TOK, 128))],
        factors,
        couple_source,
        final2,
        score2,
        scratch=[pltpu.VMEM((512, 1024), BF16), pltpu.VMEM((512, 1024), BF16)],
        flops=2_000_000_000,
    )
    mid, tokens = lax.optimization_barrier((mid, tokens))
    logits = exchange(logits, "tj")
    couple_result = call(
        pair_transition_kernel,
        shape((TOK, COLS, 128)),
        mid,
        couple_expand_matrix,
        couple_shrink_matrix,
        flops=1_000_000_000,
    )
    values = call(
        values_kernel, shape((2048, 256), BF16), tokens, mixing_content_matrix, flops=1_000_000_000
    )
    alignment_result = call(
        last_kernel,
        shape((ROWS, TOK, 64)),
        logits,
        values,
        gates,
        wf_hi,
        wf_lo,
        alignment_source,
        alignment_expand_matrix,
        alignment_shrink_matrix.T,
        scratch=[pltpu.VMEM((256, 2048), BF16), pltpu.VMEM((256, 2048), BF16)],
        flops=500_000_000,
    )
    return (alignment_result, couple_result)


def solution(mesh):
    rows, pairs = P("tj", "ti", None), P("ti", "tj", None)
    return jax.shard_map(
        shards,
        mesh=mesh,
        in_specs=(rows, pairs) + (P(),) * 10,
        out_specs=(rows, pairs),
        check_vma=False,
    )
```

```python
import functools

import jax
import jax.numpy as jnp
from jax import lax
from jax.experimental import pallas as pl
from jax.experimental.pallas import tpu as pltpu
from jax.sharding import PartitionSpec as P

F32 = jnp.float32
BF16 = jnp.bfloat16
EPS = 1e-05
TI = 8
TJ = 16
ROWS = 4
TOK = 32
COLS = 16
NN = (((1,), (0,)), ((), ()))
NT = (((1,), (1,)), ((), ()))


def dot(a, b, dims=NN):
    return lax.dot_general(a, b, dims, preferred_element_type=F32)


def split(x):
    hi = x.astype(BF16)
    return hi, (x - hi.astype(F32)).astype(BF16)


def dot3(a, b, dims=NN):
    (ah, al), (bh, bl) = a, b
    return dot(ah, bh, dims) + dot(ah, bl, dims) + dot(al, bh, dims)


def iota(shape, dim):
    return lax.broadcasted_iota(jnp.int32, shape, dim)


def normed(x):
    centred = x - jnp.mean(x, axis=-1, keepdims=True)
    var = jnp.mean(centred * centred, axis=-1, keepdims=True)
    return centred * lax.rsqrt(var + EPS)


def head_tiles(w):
    group = iota((64, 128), 1) // 32
    tiles = []
    for half in range(2):
        part = w[:, half * 128 : half * 128 + 128]
        turned = [pltpu.roll(part, 32 * d, 1) if d else part for d in range(4)]
        for q in range(4):
            tile = turned[(3 - q) % 4]
            for s in range(3):
                tile = jnp.where(group == s, turned[(s - q) % 4], tile)
            tiles.append(tile)
    return tiles


def head_weights(w):
    group = iota((64, 128), 1) // 32
    zero = jnp.zeros((64, 128), BF16)
    out = []
    for tile in head_tiles(w):
        out.append(
            tuple(
                jnp.concatenate([jnp.where(group == s, part, zero) for s in range(ROWS)], axis=0)
                for part in split(tile)
            )
        )
    return out


def first_kernel(x_ref, send_ref, own_ref):
    x = normed(x_ref[...])
    low = jnp.concatenate([x[0], x[1]], axis=1)
    high = jnp.concatenate([x[2], x[3]], axis=1)
    own_ref[:, :128] = low
    own_ref[:, 128:] = high
    for d in range(TI):
        send_ref[d, :TOK, :] = low
        send_ref[d, TOK:, :] = high


def prepare_kernel(
    own_ref, w_ref, t_ref, score_ref, wg_ref,
    left_ref, wr_hi_ref, wr_lo_ref, t_out_ref, score_out_ref, gate_ref,
):
    x = own_ref[...]
    one = split(x)
    xs = tuple(jnp.concatenate([part] * 4, axis=0) for part in one)
    ws = split(w_ref[...])
    pick = (iota((128, 64), 0) // 4 == iota((128, 64), 1)).astype(BF16)
    tile_k = (iota((64, 256), 0) == iota((64, 256), 1) % 64).astype(BF16)
    keep = iota((128, 256), 0) % 4 == iota((128, 256), 1) // 64
    wl = []
    for part in ws:
        rows = dot(pick, part, NT).astype(BF16)
        wl.append(jnp.where(keep, dot(rows, tile_k), 0.0).astype(BF16))
    prod = dot3(tuple(wl), xs, NT) * (1.0 / 64.0)
    group = iota((16, 128), 1) // 32
    for half in range(2):
        out = jnp.zeros((16, 128), F32)
        for q in range(4):
            at = half * 64 + q * 16
            out = jnp.where(group == q, prod[at : at + 16], out)
        left_ref[half * 16 : half * 16 + 16, :] = out
    tile_b = (iota((64, 128), 0) == 32 + iota((64, 128), 1) % 32).astype(BF16)
    keep_r = iota((256, 128), 0) // 64 == iota((256, 128), 1) // 32
    for part, ref in zip(ws, (wr_hi_ref, wr_lo_ref)):
        tall = jnp.concatenate([dot(part, tile_b)] * 4, axis=0)
        ref[...] = jnp.where(keep_r, tall, 0.0).astype(BF16)
    th, tl = split(t_ref[...])
    t_out_ref[:, :128] = th
    t_out_ref[:, 128:] = tl
    score = score_ref[...]
    tall = jnp.concatenate([jnp.broadcast_to(score[h : h + 1], (16, 128)) for h in range(8)], axis=0)
    sh, sl = split(tall.T)
    score_out_ref[:, :128] = sh
    score_out_ref[:, 128:] = sl
    for h, wg in enumerate(head_weights(wg_ref[...])):
        gate_ref[:, h * 128 : h * 128 + 128] = 1.0 / (1.0 + jnp.exp(-dot3(one, wg)))


def all_tokens(recv_ref):
    return (
        recv_ref[:, :TOK, :].reshape(TI * TOK, 128),
        recv_ref[:, TOK:, :].reshape(TI * TOK, 128),
    )


def right_kernel(recv_ref, left_ref, wr_hi_ref, wr_lo_ref, send_ref):
    low, high = all_tokens(recv_ref)
    wh, wl = wr_hi_ref[...], wr_lo_ref[...]
    right = dot3(split(low), (wh[:128], wl[:128])) + dot3(split(high), (wh[128:], wl[128:]))
    left = left_ref[...]
    for d in range(TJ):
        send_ref[d, :32, :] = left
        send_ref[d, 32:, :] = right[d * COLS : (d + 1) * COLS]


def values_kernel(recv_ref, wv_ref, v_ref):
    low, high = all_tokens(recv_ref)
    xs = split(jnp.concatenate([low, high], axis=1))
    for h, wv in enumerate(head_weights(wv_ref[...])):
        vh, vl = split(dot3(xs, wv))
        for d in range(TJ):
            at = (d * 8 + h) * COLS
            v_ref[at : at + COLS, :128] = vh[d * COLS : (d + 1) * COLS]
            v_ref[at : at + COLS, 128:] = vl[d * COLS : (d + 1) * COLS]


def pair_kernel(recv_ref, pair_ref, t_ref, score_ref, mid_ref, send_ref):
    rows = [
        jnp.concatenate([recv_ref[:, r, :], recv_ref[:, 16 + r, :]], axis=1) for r in range(16)
    ]
    left = jnp.concatenate(rows, axis=0).T
    lh, ll = split(left)
    left3 = jnp.concatenate([lh, lh, ll], axis=1)
    group = iota((16, 128), 1) // 32
    zero = jnp.zeros((16, 128), BF16)
    column = iota((TOK, 128), 1) % 16
    tile = jnp.zeros((TOK, 128), F32)
    fh, fl = [], []
    for pair in range(COLS // 2):
        blocks = []
        for j in (2 * pair, 2 * pair + 1):
            right = recv_ref[:, 32 + j, :]
            turned = [split(pltpu.roll(right, 32 * d, 1) if d else right) for d in range(4)]
            parts = []
            for which in range(2):
                tiles = [
                    jnp.where(group == a, turned[(a - s) % 4][which], zero)
                    for a in range(4)
                    for s in range(4)
                ]
                parts.append(jnp.concatenate(tiles, axis=0))
            blocks.append(jnp.concatenate([parts[0], parts[1], parts[0]], axis=0))
        outer = dot(left3, jnp.concatenate(blocks, axis=1))
        oh, ol = split(outer)
        for q in range(2):
            for part, keep in ((oh, fh), (ol, fl)):
                keep.append(
                    jnp.concatenate(
                        [part[g * 32 : g * 32 + 32, q * 128 : q * 128 + 128] for g in range(8)], axis=1
                    )
                )
    wide = dot(jnp.concatenate(fh, axis=0), t_ref[...])
    update = wide[:, :128] + wide[:, 128:] + dot(jnp.concatenate(fl, axis=0), t_ref[:, :128])
    normal = []
    for j in range(COLS):
        mid = pair_ref[:, j, :] + update[j * TOK : (j + 1) * TOK]
        mid_ref[j] = mid
        normal.append(normed(mid))
    nh, nl = split(jnp.concatenate(normal, axis=0))
    wide = dot(nh, score_ref[...])
    logits = wide[:, :128] + wide[:, 128:] + dot(nl, score_ref[:, :128])
    for j in range(COLS):
        tile = jnp.where(column == j, logits[j * TOK : (j + 1) * TOK], tile)
    for d in range(TJ):
        send_ref[d] = tile


def pair_transition_kernel(mid_ref, expand_ref, shrink_ref, out_ref):
    eh, el = split(expand_ref[...])
    expand3 = jnp.concatenate([eh, eh, el], axis=0)
    sh, sl = split(shrink_ref[...])
    shrink2 = jnp.concatenate([sh, sl], axis=1)
    step = 4
    for at in range(0, COLS, step):
        mid = mid_ref[at : at + step].reshape(step * TOK, 128)
        nh, nl = split(normed(mid))
        hidden = dot(jnp.concatenate([nh, nl, nh], axis=1), expand3)
        gate = hidden[:, :512]
        act = gate / (1.0 + jnp.exp(-gate)) * hidden[:, 512:]
        ah, al = split(act)
        wide = dot(ah, shrink2)
        out = mid + wide[:, :128] + wide[:, 128:] + dot(al, sh)
        for j in range(step):
            out_ref[:, at + j, :] = out[j * TOK : (j + 1) * TOK]


def group_all(x, op):
    lane = iota(x.shape, 1)
    for d in (8, 4, 2, 1):
        other = jnp.where((lane & d) == 0, pltpu.roll(x, 128 - d, 1), pltpu.roll(x, d, 1))
        x = op(x, other)
    return x


def three(a, b):
    (ah, al), (bh, bl) = a, b
    return dot(jnp.concatenate([ah, ah, al], axis=1), jnp.concatenate([bh, bl, bh], axis=1), NT)


def swap_groups(tiles):
    group = iota(tiles[0].shape, 1) // 32
    for d in (2, 1):
        low = (group & d) == 0
        out = list(tiles)
        for t in range(4):
            if t & d == 0:
                a, b = tiles[t], tiles[t | d]
                out[t] = jnp.where(low, a, pltpu.roll(b, 32 * d, 1))
                out[t | d] = jnp.where(low, pltpu.roll(a, 128 - 32 * d, 1), b)
        tiles = out
    return tiles


def last_kernel(
    recv_ref, v_ref, gate_ref, wf_ref, x_ref, expand_ref, shrink_ref, out_ref, w_hi, w_lo
):
    top = recv_ref[0]
    for d in range(1, TJ):
        top = jnp.maximum(top, recv_ref[d])
    top = group_all(top, jnp.maximum)
    terms = [jnp.exp(recv_ref[d] - top) for d in range(TJ)]
    total = terms[0]
    for d in range(1, TJ):
        total = total + terms[d]
    inv = 1.0 / group_all(total, jnp.add)
    head = iota((TOK, 128), 1) // 16
    zero = jnp.zeros((TOK, 128), BF16)
    for d in range(TJ):
        wh, wl = split(terms[d])
        for h in range(8):
            w_hi[h * TOK : (h + 1) * TOK, d * 128 : d * 128 + 128] = jnp.where(head == h, wh, zero)
            w_lo[h * TOK : (h + 1) * TOK, d * 128 : d * 128 + 128] = jnp.where(head == h, wl, zero)
    wide = dot(w_hi[...], v_ref[...])
    mixed = wide[:, :128] + wide[:, 128:] + dot(w_lo[...], v_ref[:, :128])
    gated = [
        mixed[h * TOK : (h + 1) * TOK]
        * (gate_ref[:, h * 128 : h * 128 + 128] * inv[:, h * 16 : h * 16 + 1])
        for h in range(8)
    ]
    halves = [swap_groups(gated[:4]), swap_groups(gated[4:])]
    rows = jnp.concatenate(
        [jnp.concatenate([halves[0][s], halves[1][s]], axis=1) for s in range(ROWS)], axis=0
    )
    mid = x_ref[...].reshape(ROWS * TOK, 64) + three(split(rows), split(wf_ref[...]))
    nh, nl = split(normed(mid))
    eh, el = split(expand_ref[...])
    hidden = dot(jnp.concatenate([nh, nl, nh], axis=1), jnp.concatenate([eh, eh, el], axis=0))
    gate = hidden[:, :256]
    act = gate / (1.0 + jnp.exp(-gate)) * hidden[:, 256:]
    ah, al = split(act)
    sh, sl = split(shrink_ref[...])
    out = mid + dot(
        jnp.concatenate([ah, ah, al], axis=1), jnp.concatenate([sh, sl, sh], axis=1), NT
    )
    out_ref[...] = out.reshape(ROWS, TOK, 64)


def call(kernel, outs, *args, specs=None, scratch=(), flops=0):
    vmem = pl.BlockSpec(memory_space=pltpu.VMEM)
    in_specs = [vmem] * len(args) if specs is None else [s or vmem for s in specs]
    single = not isinstance(outs, (list, tuple))
    outs = [outs] if single else list(outs)
    moved = sum(a.size * a.dtype.itemsize for a in args) + sum(
        o.size * o.dtype.itemsize for o in outs
    )
    res = pl.pallas_call(
        kernel,
        out_shape=outs,
        in_specs=in_specs,
        out_specs=[vmem] * len(outs),
        scratch_shapes=list(scratch),
        compiler_params=pltpu.CompilerParams(vmem_limit_bytes=24 << 20),
        cost_estimate=pl.CostEstimate(flops=flops, bytes_accessed=moved, transcendentals=0),
    )(*args)
    return res[0] if single else res


def shape(dims, dtype=F32):
    return jax.ShapeDtypeStruct(dims, dtype)


def shards(
    alignment_source,
    couple_source,
    tensor_operand_matrix,
    tensor_final_matrix,
    mixing_content_matrix,
    mixing_switch_matrix,
    mixing_score_matrix,
    mixing_final_matrix,
    alignment_expand_matrix,
    alignment_shrink_matrix,
    couple_expand_matrix,
    couple_shrink_matrix,
):
    exchange = functools.partial(lax.all_to_all, split_axis=0, concat_axis=0, tiled=True)
    send, own = call(first_kernel, [shape((TI, 64, 128)), shape((TOK, 256))], alignment_source)
    tokens = exchange(send, "ti")
    prepared = call(
        prepare_kernel,
        [shape((32, 128)), shape((256, 128), BF16), shape((256, 128), BF16)]
        + [shape((1024, 256), BF16), shape((128, 256), BF16), shape((32, 1024))],
        own,
        tensor_operand_matrix,
        tensor_final_matrix,
        mixing_score_matrix.T,
        mixing_switch_matrix,
        flops=500_000_000,
    )
    left, wr_hi, wr_lo, final2, score2, gates = prepared
    factors = call(right_kernel, shape((TJ, 48, 128)), tokens, left, wr_hi, wr_lo)
    factors = exchange(factors, "tj")
    mid, logits = call(
        pair_kernel,
        [shape((COLS, TOK, 128)), shape((TJ, TOK, 128))],
        factors,
        couple_source,
        final2,
        score2,
        flops=2_000_000_000,
    )
    mid, tokens = lax.optimization_barrier((mid, tokens))
    logits = exchange(logits, "tj")
    couple_result = call(
        pair_transition_kernel,
        shape((TOK, COLS, 128)),
        mid,
        couple_expand_matrix,
        couple_shrink_matrix,
        flops=1_000_000_000,
    )
    values = call(
        values_kernel, shape((2048, 256), BF16), tokens, mixing_content_matrix, flops=1_000_000_000
    )
    alignment_result = call(
        last_kernel,
        shape((ROWS, TOK, 64)),
        logits,
        values,
        gates,
        mixing_final_matrix.T,
        alignment_source,
        alignment_expand_matrix,
        alignment_shrink_matrix.T,
        scratch=[pltpu.VMEM((256, 2048), BF16), pltpu.VMEM((256, 2048), BF16)],
        flops=500_000_000,
    )
    return (alignment_result, couple_result)


def solution(mesh):
    rows, pairs = P("tj", "ti", None), P("ti", "tj", None)
    return jax.shard_map(
        shards,
        mesh=mesh,
        in_specs=(rows, pairs) + (P(),) * 10,
        out_specs=(rows, pairs),
        check_vma=False,
    )
```

```python
import functools

import jax
import jax.numpy as jnp
from jax import lax
from jax.experimental import pallas as pl
from jax.experimental.pallas import tpu as pltpu
from jax.sharding import PartitionSpec as P

F32 = jnp.float32
BF16 = jnp.bfloat16
EPS = 1e-05
TI = 8
TJ = 16
ROWS = 4
TOK = 32
COLS = 16
NN = (((1,), (0,)), ((), ()))
NT = (((1,), (1,)), ((), ()))


def dot(a, b, dims=NN):
    return lax.dot_general(a, b, dims, preferred_element_type=F32)


def split(x):
    hi = x.astype(BF16)
    return hi, (x - hi.astype(F32)).astype(BF16)


def dot3(a, b, dims=NN):
    (ah, al), (bh, bl) = a, b
    return dot(ah, bh, dims) + dot(ah, bl, dims) + dot(al, bh, dims)


def iota(shape, dim):
    return lax.broadcasted_iota(jnp.int32, shape, dim)


def normed(x):
    centred = x - jnp.mean(x, axis=-1, keepdims=True)
    var = jnp.mean(centred * centred, axis=-1, keepdims=True)
    return centred * lax.rsqrt(var + EPS)


def head_tiles(w):
    group = iota((64, 128), 1) // 32
    tiles = []
    for half in range(2):
        part = w[:, half * 128 : half * 128 + 128]
        turned = [pltpu.roll(part, 32 * d, 1) if d else part for d in range(4)]
        for q in range(4):
            tile = turned[(3 - q) % 4]
            for s in range(3):
                tile = jnp.where(group == s, turned[(s - q) % 4], tile)
            tiles.append(tile)
    return tiles


def head_weights(w):
    group = iota((64, 128), 1) // 32
    zero = jnp.zeros((64, 128), BF16)
    out = []
    for tile in head_tiles(w):
        out.append(
            tuple(
                jnp.concatenate([jnp.where(group == s, part, zero) for s in range(ROWS)], axis=0)
                for part in split(tile)
            )
        )
    return out


def first_kernel(x_ref, send_ref, own_ref):
    x = normed(x_ref[...])
    low = jnp.concatenate([x[0], x[1]], axis=1)
    high = jnp.concatenate([x[2], x[3]], axis=1)
    own_ref[:, :128] = low
    own_ref[:, 128:] = high
    for d in range(TI):
        send_ref[d, :TOK, :] = low
        send_ref[d, TOK:, :] = high


def all_tokens(recv_ref):
    return (
        recv_ref[:, :TOK, :].reshape(TI * TOK, 128),
        recv_ref[:, TOK:, :].reshape(TI * TOK, 128),
    )


def factors_kernel(recv_ref, own_ref, w_ref, send_ref):
    w = w_ref[...]
    group = iota((64, 128), 1) // 32
    twice = jnp.concatenate([w, w], axis=1)
    wide = split(jnp.where(group % 2 == 1, twice, pltpu.roll(twice, 96, 1)))
    zero = jnp.zeros((64, 128), BF16)
    wr = [[jnp.where(group == s, part, zero) for s in range(ROWS)] for part in wide]
    low, high = (split(x) for x in all_tokens(recv_ref))
    wr_low = tuple(jnp.concatenate(tiles[:2], axis=0) for tiles in wr)
    wr_high = tuple(jnp.concatenate(tiles[2:], axis=0) for tiles in wr)
    right = dot3(low, wr_low) + dot3(high, wr_high)
    xs = tuple(jnp.concatenate([part] * 4, axis=0) for part in split(own_ref[...]))
    pick = (iota((128, 64), 0) // 4 == iota((128, 64), 1)).astype(BF16)
    keep = iota((128, 256), 0) % 4 == iota((128, 256), 1) // 64
    wl = []
    for part in split(w):
        rows = dot(pick, part, NT)
        wl.append(jnp.where(keep, jnp.concatenate([rows] * 4, axis=1), 0.0).astype(BF16))
    prod = dot3(tuple(wl), xs, NT) * (1.0 / 64.0)
    group = iota((16, 128), 1) // 32
    left = []
    for half in range(2):
        out = jnp.zeros((16, 128), F32)
        for q in range(4):
            at = half * 64 + q * 16
            out = jnp.where(group == q, prod[at : at + 16], out)
        left.append(out)
    for d in range(TJ):
        send_ref[d, :16, :] = left[0]
        send_ref[d, 16:32, :] = left[1]
        send_ref[d, 32:, :] = right[d * COLS : (d + 1) * COLS]


def values_kernel(recv_ref, wv_ref, own_ref, wg_ref, v_ref, gate_ref):
    own = split(own_ref[...])
    for h, wg in enumerate(head_weights(wg_ref[...])):
        gate_ref[:, h * 128 : h * 128 + 128] = 1.0 / (1.0 + jnp.exp(-dot3(own, wg)))
    low, high = all_tokens(recv_ref)
    xs = split(jnp.concatenate([low, high], axis=1))
    for h, wv in enumerate(head_weights(wv_ref[...])):
        vh, vl = split(dot3(xs, wv))
        for d in range(TJ):
            at = (d * 8 + h) * COLS
            v_ref[at : at + COLS, :128] = vh[d * COLS : (d + 1) * COLS]
            v_ref[at : at + COLS, 128:] = vl[d * COLS : (d + 1) * COLS]


def pair_kernel(recv_ref, pair_ref, t_ref, score_ref, mid_ref, send_ref):
    rows = [
        jnp.concatenate([recv_ref[:, r, :], recv_ref[:, 16 + r, :]], axis=1) for r in range(16)
    ]
    left = jnp.concatenate(rows, axis=0).T
    lh, ll = split(left)
    left3 = jnp.concatenate([lh, lh, ll], axis=1)
    group = iota((16, 128), 1) // 32
    zero = jnp.zeros((16, 128), BF16)
    column = iota((TOK, 128), 1) % 16
    tile = jnp.zeros((TOK, 128), F32)
    th, tl = split(t_ref[...])
    fh, fl = [], []
    for pair in range(COLS // 2):
        blocks = []
        for j in (2 * pair, 2 * pair + 1):
            right = recv_ref[:, 32 + j, :]
            turned = [split(pltpu.roll(right, 32 * d, 1) if d else right) for d in range(4)]
            parts = []
            for which in range(2):
                tiles = [
                    jnp.where(group == a, turned[(a - s) % 4][which], zero)
                    for a in range(4)
                    for s in range(4)
                ]
                parts.append(jnp.concatenate(tiles, axis=0))
            blocks.append(jnp.concatenate([parts[0], parts[1], parts[0]], axis=0))
        outer = dot(left3, jnp.concatenate(blocks, axis=1))
        oh, ol = split(outer)
        for q in range(2):
            for part, keep in ((oh, fh), (ol, fl)):
                keep.append(
                    jnp.concatenate(
                        [part[g * 32 : g * 32 + 32, q * 128 : q * 128 + 128] for g in range(8)], axis=1
                    )
                )
    wide = dot(jnp.concatenate(fh, axis=0), jnp.concatenate([th, tl], axis=1))
    update = wide[:, :128] + wide[:, 128:] + dot(jnp.concatenate(fl, axis=0), th)
    normal = []
    for j in range(COLS):
        mid = pair_ref[:, j, :] + update[j * TOK : (j + 1) * TOK]
        mid_ref[j] = mid
        normal.append(normed(mid))
    nh, nl = split(jnp.concatenate(normal, axis=0))
    score = score_ref[...]
    score = [jnp.broadcast_to(score[h : h + 1], (16, 128)) for h in range(8)]
    logits = dot3((nh, nl), split(jnp.concatenate(score, axis=0)), NT)
    for j in range(COLS):
        tile = jnp.where(column == j, logits[j * TOK : (j + 1) * TOK], tile)
    for d in range(TJ):
        send_ref[d] = tile


def pair_transition_kernel(mid_ref, expand_ref, shrink_ref, out_ref):
    eh, el = split(expand_ref[...])
    expand3 = jnp.concatenate([eh, eh, el], axis=0)
    sh, sl = split(shrink_ref[...])
    shrink2 = jnp.concatenate([sh, sl], axis=1)
    step = 4
    for at in range(0, COLS, step):
        mid = mid_ref[at : at + step].reshape(step * TOK, 128)
        nh, nl = split(normed(mid))
        hidden = dot(jnp.concatenate([nh, nl, nh], axis=1), expand3)
        gate = hidden[:, :512]
        act = gate / (1.0 + jnp.exp(-gate)) * hidden[:, 512:]
        ah, al = split(act)
        wide = dot(ah, shrink2)
        out = mid + wide[:, :128] + wide[:, 128:] + dot(al, sh)
        for j in range(step):
            out_ref[:, at + j, :] = out[j * TOK : (j + 1) * TOK]


def group_all(x, op):
    lane = iota(x.shape, 1)
    for d in (8, 4, 2, 1):
        other = jnp.where((lane & d) == 0, pltpu.roll(x, 128 - d, 1), pltpu.roll(x, d, 1))
        x = op(x, other)
    return x


def three(a, b):
    (ah, al), (bh, bl) = a, b
    return dot(jnp.concatenate([ah, ah, al], axis=1), jnp.concatenate([bh, bl, bh], axis=1), NT)


def swap_groups(tiles):
    group = iota(tiles[0].shape, 1) // 32
    for d in (2, 1):
        low = (group & d) == 0
        out = list(tiles)
        for t in range(4):
            if t & d == 0:
                a, b = tiles[t], tiles[t | d]
                out[t] = jnp.where(low, a, pltpu.roll(b, 32 * d, 1))
                out[t | d] = jnp.where(low, pltpu.roll(a, 128 - 32 * d, 1), b)
        tiles = out
    return tiles


def last_kernel(
    recv_ref, v_ref, gate_ref, wf_ref, x_ref, expand_ref, shrink_ref, out_ref, w_hi, w_lo
):
    top = recv_ref[0]
    for d in range(1, TJ):
        top = jnp.maximum(top, recv_ref[d])
    top = group_all(top, jnp.maximum)
    terms = [jnp.exp(recv_ref[d] - top) for d in range(TJ)]
    total = terms[0]
    for d in range(1, TJ):
        total = total + terms[d]
    inv = 1.0 / group_all(total, jnp.add)
    head = iota((TOK, 128), 1) // 16
    zero = jnp.zeros((TOK, 128), BF16)
    for d in range(TJ):
        wh, wl = split(terms[d])
        for h in range(8):
            w_hi[h * TOK : (h + 1) * TOK, d * 128 : d * 128 + 128] = jnp.where(head == h, wh, zero)
            w_lo[h * TOK : (h + 1) * TOK, d * 128 : d * 128 + 128] = jnp.where(head == h, wl, zero)
    wide = dot(w_hi[...], v_ref[...])
    mixed = wide[:, :128] + wide[:, 128:] + dot(w_lo[...], v_ref[:, :128])
    gated = [
        mixed[h * TOK : (h + 1) * TOK]
        * (gate_ref[:, h * 128 : h * 128 + 128] * inv[:, h * 16 : h * 16 + 1])
        for h in range(8)
    ]
    halves = [swap_groups(gated[:4]), swap_groups(gated[4:])]
    rows = jnp.concatenate(
        [jnp.concatenate([halves[0][s], halves[1][s]], axis=1) for s in range(ROWS)], axis=0
    )
    mid = x_ref[...].reshape(ROWS * TOK, 64) + three(split(rows), split(wf_ref[...]))
    nh, nl = split(normed(mid))
    eh, el = split(expand_ref[...])
    hidden = dot(jnp.concatenate([nh, nl, nh], axis=1), jnp.concatenate([eh, eh, el], axis=0))
    gate = hidden[:, :256]
    act = gate / (1.0 + jnp.exp(-gate)) * hidden[:, 256:]
    ah, al = split(act)
    sh, sl = split(shrink_ref[...])
    out = mid + dot(
        jnp.concatenate([ah, ah, al], axis=1), jnp.concatenate([sh, sl, sh], axis=1), NT
    )
    out_ref[...] = out.reshape(ROWS, TOK, 64)


def call(kernel, outs, *args, specs=None, scratch=(), flops=0):
    vmem = pl.BlockSpec(memory_space=pltpu.VMEM)
    in_specs = [vmem] * len(args) if specs is None else [s or vmem for s in specs]
    single = not isinstance(outs, (list, tuple))
    outs = [outs] if single else list(outs)
    moved = sum(a.size * a.dtype.itemsize for a in args) + sum(
        o.size * o.dtype.itemsize for o in outs
    )
    res = pl.pallas_call(
        kernel,
        out_shape=outs,
        in_specs=in_specs,
        out_specs=[vmem] * len(outs),
        scratch_shapes=list(scratch),
        compiler_params=pltpu.CompilerParams(vmem_limit_bytes=24 << 20),
        cost_estimate=pl.CostEstimate(flops=flops, bytes_accessed=moved, transcendentals=0),
    )(*args)
    return res[0] if single else res


def shape(dims, dtype=F32):
    return jax.ShapeDtypeStruct(dims, dtype)


def shards(
    alignment_source,
    couple_source,
    tensor_operand_matrix,
    tensor_final_matrix,
    mixing_content_matrix,
    mixing_switch_matrix,
    mixing_score_matrix,
    mixing_final_matrix,
    alignment_expand_matrix,
    alignment_shrink_matrix,
    couple_expand_matrix,
    couple_shrink_matrix,
):
    exchange = functools.partial(lax.all_to_all, split_axis=0, concat_axis=0, tiled=True)
    send, own = call(first_kernel, [shape((TI, 64, 128)), shape((TOK, 256))], alignment_source)
    tokens = exchange(send, "ti")
    factors = call(factors_kernel, shape((TJ, 48, 128)), tokens, own, tensor_operand_matrix)
    factors = exchange(factors, "tj")
    mid, logits = call(
        pair_kernel,
        [shape((COLS, TOK, 128)), shape((TJ, TOK, 128))],
        factors,
        couple_source,
        tensor_final_matrix,
        mixing_score_matrix.T,
        flops=2_000_000_000,
    )
    mid, tokens = lax.optimization_barrier((mid, tokens))
    logits = exchange(logits, "tj")
    couple_result = call(
        pair_transition_kernel,
        shape((TOK, COLS, 128)),
        mid,
        couple_expand_matrix,
        couple_shrink_matrix,
        flops=1_000_000_000,
    )
    values, gates = call(
        values_kernel,
        [shape((2048, 256), BF16), shape((TOK, 1024))],
        tokens,
        mixing_content_matrix,
        own,
        mixing_switch_matrix,
        flops=1_000_000_000,
    )
    alignment_result = call(
        last_kernel,
        shape((ROWS, TOK, 64)),
        logits,
        values,
        gates,
        mixing_final_matrix.T,
        alignment_source,
        alignment_expand_matrix,
        alignment_shrink_matrix.T,
        scratch=[pltpu.VMEM((256, 2048), BF16), pltpu.VMEM((256, 2048), BF16)],
        flops=500_000_000,
    )
    return (alignment_result, couple_result)


def solution(mesh):
    rows, pairs = P("tj", "ti", None), P("ti", "tj", None)
    return jax.shard_map(
        shards,
        mesh=mesh,
        in_specs=(rows, pairs) + (P(),) * 10,
        out_specs=(rows, pairs),
        check_vma=False,
    )
```

```python
import jax
import jax.numpy as jnp
from jax import lax
from jax.experimental import pallas as pl
from jax.experimental.pallas import tpu as pltpu
from jax.sharding import PartitionSpec as P

F32 = jnp.float32
BF16 = jnp.bfloat16
EPS = 1e-05
TI = 8
TJ = 16
ROWS = 4
TOK = 32
COLS = 16
ORDER_TI = [k ^ 3 for k in range(8)]
ORDER_TJ = [k ^ 11 for k in range(16)]
NN = (((1,), (0,)), ((), ()))
NT = (((1,), (1,)), ((), ()))


def dot(a, b, dims=NN):
    return lax.dot_general(a, b, dims, preferred_element_type=F32)


def split(x):
    hi = x.astype(BF16)
    return hi, (x - hi.astype(F32)).astype(BF16)


def dot3(a, b, dims=NN):
    (ah, al), (bh, bl) = a, b
    return dot(ah, bh, dims) + dot(ah, bl, dims) + dot(al, bh, dims)


def iota(shape, dim):
    return lax.broadcasted_iota(jnp.int32, shape, dim)


def normed(x):
    centred = x - jnp.mean(x, axis=-1, keepdims=True)
    var = jnp.mean(centred * centred, axis=-1, keepdims=True)
    return centred * lax.rsqrt(var + EPS)


def head_tiles(w):
    group = iota((64, 128), 1) // 32
    tiles = []
    for half in range(2):
        part = w[:, half * 128 : half * 128 + 128]
        turned = [pltpu.roll(part, 32 * d, 1) if d else part for d in range(4)]
        for q in range(4):
            tile = turned[(3 - q) % 4]
            for s in range(3):
                tile = jnp.where(group == s, turned[(s - q) % 4], tile)
            tiles.append(tile)
    return tiles


def head_weights(w):
    group = iota((64, 128), 1) // 32
    zero = jnp.zeros((64, 128), BF16)
    out = []
    for tile in head_tiles(w):
        out.append(
            tuple(
                jnp.concatenate([jnp.where(group == s, part, zero) for s in range(ROWS)], axis=0)
                for part in split(tile)
            )
        )
    return out


def first_kernel(x_ref, send_ref, own_ref):
    x = normed(x_ref[...])
    low = jnp.concatenate([x[0], x[1]], axis=1)
    high = jnp.concatenate([x[2], x[3]], axis=1)
    own_ref[:, :128] = low
    own_ref[:, 128:] = high
    for d in range(TI):
        send_ref[d, :TOK, :] = low
        send_ref[d, TOK:, :] = high


def all_tokens(recv_ref):
    slots = [ORDER_TI.index(d) for d in range(TI)]
    return (
        jnp.concatenate([recv_ref[k, :TOK, :] for k in slots], axis=0),
        jnp.concatenate([recv_ref[k, TOK:, :] for k in slots], axis=0),
    )


def factors_kernel(recv_ref, own_ref, w_ref, send_ref):
    w = w_ref[...]
    group = iota((64, 128), 1) // 32
    twice = jnp.concatenate([w, w], axis=1)
    wide = split(jnp.where(group % 2 == 1, twice, pltpu.roll(twice, 96, 1)))
    zero = jnp.zeros((64, 128), BF16)
    wr = [[jnp.where(group == s, part, zero) for s in range(ROWS)] for part in wide]
    low, high = (split(x) for x in all_tokens(recv_ref))
    wr_low = tuple(jnp.concatenate(tiles[:2], axis=0) for tiles in wr)
    wr_high = tuple(jnp.concatenate(tiles[2:], axis=0) for tiles in wr)
    right = dot3(low, wr_low) + dot3(high, wr_high)
    xs = tuple(jnp.concatenate([part] * 4, axis=0) for part in split(own_ref[...]))
    pick = (iota((128, 64), 0) // 4 == iota((128, 64), 1)).astype(BF16)
    keep = iota((128, 256), 0) % 4 == iota((128, 256), 1) // 64
    wl = []
    for part in split(w):
        rows = dot(pick, part, NT)
        wl.append(jnp.where(keep, jnp.concatenate([rows] * 4, axis=1), 0.0).astype(BF16))
    prod = dot3(tuple(wl), xs, NT) * (1.0 / 64.0)
    group = iota((16, 128), 1) // 32
    left = []
    for half in range(2):
        out = jnp.zeros((16, 128), F32)
        for q in range(4):
            at = half * 64 + q * 16
            out = jnp.where(group == q, prod[at : at + 16], out)
        left.append(out)
    for d in range(TJ):
        send_ref[d, :16, :] = left[0]
        send_ref[d, 16:32, :] = left[1]
        at = ORDER_TJ[d] * COLS
        send_ref[d, 32:, :] = right[at : at + COLS]


def values_kernel(recv_ref, wv_ref, own_ref, wg_ref, v_ref, gate_ref):
    own = split(own_ref[...])
    for h, wg in enumerate(head_weights(wg_ref[...])):
        gate_ref[:, h * 128 : h * 128 + 128] = 1.0 / (1.0 + jnp.exp(-dot3(own, wg)))
    low, high = all_tokens(recv_ref)
    xs = split(jnp.concatenate([low, high], axis=1))
    for h, wv in enumerate(head_weights(wv_ref[...])):
        vh, vl = split(dot3(xs, wv))
        for d in range(TJ):
            at, of = (d * 8 + h) * COLS, ORDER_TJ[d] * COLS
            v_ref[at : at + COLS, :128] = vh[of : of + COLS]
            v_ref[at : at + COLS, 128:] = vl[of : of + COLS]


def pair_kernel(recv_ref, pair_ref, t_ref, score_ref, mid_ref, send_ref):
    rows = [
        jnp.concatenate([recv_ref[:, r, :], recv_ref[:, 16 + r, :]], axis=1) for r in range(16)
    ]
    left = jnp.concatenate(rows, axis=0).T
    lh, ll = split(left)
    left3 = jnp.concatenate([lh, lh, ll], axis=1)
    group = iota((16, 128), 1) // 32
    zero = jnp.zeros((16, 128), BF16)
    column = iota((TOK, 128), 1) % 16
    tile = jnp.zeros((TOK, 128), F32)
    th, tl = split(t_ref[...])
    fh, fl = [], []
    for pair in range(COLS // 2):
        blocks = []
        for j in (2 * pair, 2 * pair + 1):
            right = recv_ref[:, 32 + j, :]
            turned = [split(pltpu.roll(right, 32 * d, 1) if d else right) for d in range(4)]
            parts = []
            for which in range(2):
                tiles = [
                    jnp.where(group == a, turned[(a - s) % 4][which], zero)
                    for a in range(4)
                    for s in range(4)
                ]
                parts.append(jnp.concatenate(tiles, axis=0))
            blocks.append(jnp.concatenate([parts[0], parts[1], parts[0]], axis=0))
        outer = dot(left3, jnp.concatenate(blocks, axis=1))
        oh, ol = split(outer)
        for q in range(2):
            for part, keep in ((oh, fh), (ol, fl)):
                keep.append(
                    jnp.concatenate(
                        [part[g * 32 : g * 32 + 32, q * 128 : q * 128 + 128] for g in range(8)], axis=1
                    )
                )
    wide = dot(jnp.concatenate(fh, axis=0), jnp.concatenate([th, tl], axis=1))
    update = wide[:, :128] + wide[:, 128:] + dot(jnp.concatenate(fl, axis=0), th)
    normal = []
    for j in range(COLS):
        mid = pair_ref[:, j, :] + update[j * TOK : (j + 1) * TOK]
        mid_ref[j] = mid
        normal.append(normed(mid))
    nh, nl = split(jnp.concatenate(normal, axis=0))
    score = score_ref[...]
    score = [jnp.broadcast_to(score[h : h + 1], (16, 128)) for h in range(8)]
    logits = dot3((nh, nl), split(jnp.concatenate(score, axis=0)), NT)
    for j in range(COLS):
        tile = jnp.where(column == j, logits[j * TOK : (j + 1) * TOK], tile)
    for d in range(TJ):
        send_ref[d] = tile


def pair_transition_kernel(mid_ref, expand_ref, shrink_ref, out_ref):
    eh, el = split(expand_ref[...])
    expand3 = jnp.concatenate([eh, eh, el], axis=0)
    sh, sl = split(shrink_ref[...])
    shrink2 = jnp.concatenate([sh, sl], axis=1)
    step = 4
    for at in range(0, COLS, step):
        mid = mid_ref[at : at + step].reshape(step * TOK, 128)
        nh, nl = split(normed(mid))
        hidden = dot(jnp.concatenate([nh, nl, nh], axis=1), expand3)
        gate = hidden[:, :512]
        act = gate / (1.0 + jnp.exp(-gate)) * hidden[:, 512:]
        ah, al = split(act)
        wide = dot(ah, shrink2)
        out = mid + wide[:, :128] + wide[:, 128:] + dot(al, sh)
        for j in range(step):
            out_ref[:, at + j, :] = out[j * TOK : (j + 1) * TOK]


def group_all(x, op):
    lane = iota(x.shape, 1)
    for d in (8, 4, 2, 1):
        other = jnp.where((lane & d) == 0, pltpu.roll(x, 128 - d, 1), pltpu.roll(x, d, 1))
        x = op(x, other)
    return x


def three(a, b):
    (ah, al), (bh, bl) = a, b
    return dot(jnp.concatenate([ah, ah, al], axis=1), jnp.concatenate([bh, bl, bh], axis=1), NT)


def swap_groups(tiles):
    group = iota(tiles[0].shape, 1) // 32
    for d in (2, 1):
        low = (group & d) == 0
        out = list(tiles)
        for t in range(4):
            if t & d == 0:
                a, b = tiles[t], tiles[t | d]
                out[t] = jnp.where(low, a, pltpu.roll(b, 32 * d, 1))
                out[t | d] = jnp.where(low, pltpu.roll(a, 128 - 32 * d, 1), b)
        tiles = out
    return tiles


def last_kernel(
    recv_ref, v_ref, gate_ref, wf_ref, x_ref, expand_ref, shrink_ref, out_ref, w_hi, w_lo
):
    top = recv_ref[0]
    for d in range(1, TJ):
        top = jnp.maximum(top, recv_ref[d])
    top = group_all(top, jnp.maximum)
    terms = [jnp.exp(recv_ref[d] - top) for d in range(TJ)]
    total = terms[0]
    for d in range(1, TJ):
        total = total + terms[d]
    inv = 1.0 / group_all(total, jnp.add)
    head = iota((TOK, 128), 1) // 16
    zero = jnp.zeros((TOK, 128), BF16)
    for d in range(TJ):
        wh, wl = split(terms[d])
        for h in range(8):
            w_hi[h * TOK : (h + 1) * TOK, d * 128 : d * 128 + 128] = jnp.where(head == h, wh, zero)
            w_lo[h * TOK : (h + 1) * TOK, d * 128 : d * 128 + 128] = jnp.where(head == h, wl, zero)
    wide = dot(w_hi[...], v_ref[...])
    mixed = wide[:, :128] + wide[:, 128:] + dot(w_lo[...], v_ref[:, :128])
    gated = [
        mixed[h * TOK : (h + 1) * TOK]
        * (gate_ref[:, h * 128 : h * 128 + 128] * inv[:, h * 16 : h * 16 + 1])
        for h in range(8)
    ]
    halves = [swap_groups(gated[:4]), swap_groups(gated[4:])]
    rows = jnp.concatenate(
        [jnp.concatenate([halves[0][s], halves[1][s]], axis=1) for s in range(ROWS)], axis=0
    )
    mid = x_ref[...].reshape(ROWS * TOK, 64) + three(split(rows), split(wf_ref[...]))
    nh, nl = split(normed(mid))
    eh, el = split(expand_ref[...])
    hidden = dot(jnp.concatenate([nh, nl, nh], axis=1), jnp.concatenate([eh, eh, el], axis=0))
    gate = hidden[:, :256]
    act = gate / (1.0 + jnp.exp(-gate)) * hidden[:, 256:]
    ah, al = split(act)
    sh, sl = split(shrink_ref[...])
    out = mid + dot(
        jnp.concatenate([ah, ah, al], axis=1), jnp.concatenate([sh, sl, sh], axis=1), NT
    )
    out_ref[...] = out.reshape(ROWS, TOK, 64)


def call(kernel, outs, *args, specs=None, scratch=(), flops=0):
    vmem = pl.BlockSpec(memory_space=pltpu.VMEM)
    in_specs = [vmem] * len(args) if specs is None else [s or vmem for s in specs]
    single = not isinstance(outs, (list, tuple))
    outs = [outs] if single else list(outs)
    moved = sum(a.size * a.dtype.itemsize for a in args) + sum(
        o.size * o.dtype.itemsize for o in outs
    )
    res = pl.pallas_call(
        kernel,
        out_shape=outs,
        in_specs=in_specs,
        out_specs=[vmem] * len(outs),
        scratch_shapes=list(scratch),
        compiler_params=pltpu.CompilerParams(vmem_limit_bytes=24 << 20),
        cost_estimate=pl.CostEstimate(flops=flops, bytes_accessed=moved, transcendentals=0),
    )(*args)
    return res[0] if single else res


def shape(dims, dtype=F32):
    return jax.ShapeDtypeStruct(dims, dtype)


def exchange(x, axis, order):
    return lax.all_to_all(x, axis, 0, 0, axis_index_groups=[order], tiled=True)


def shards(
    alignment_source,
    couple_source,
    tensor_operand_matrix,
    tensor_final_matrix,
    mixing_content_matrix,
    mixing_switch_matrix,
    mixing_score_matrix,
    mixing_final_matrix,
    alignment_expand_matrix,
    alignment_shrink_matrix,
    couple_expand_matrix,
    couple_shrink_matrix,
):
    send, own = call(first_kernel, [shape((TI, 64, 128)), shape((TOK, 256))], alignment_source)
    tokens = exchange(send, "ti", ORDER_TI)
    factors = call(factors_kernel, shape((TJ, 48, 128)), tokens, own, tensor_operand_matrix)
    factors = exchange(factors, "tj", ORDER_TJ)
    mid, logits = call(
        pair_kernel,
        [shape((COLS, TOK, 128)), shape((TJ, TOK, 128))],
        factors,
        couple_source,
        tensor_final_matrix,
        mixing_score_matrix.T,
        flops=2_000_000_000,
    )
    mid, tokens = lax.optimization_barrier((mid, tokens))
    logits = exchange(logits, "tj", ORDER_TJ)
    couple_result = call(
        pair_transition_kernel,
        shape((TOK, COLS, 128)),
        mid,
        couple_expand_matrix,
        couple_shrink_matrix,
        flops=1_000_000_000,
    )
    values, gates = call(
        values_kernel,
        [shape((2048, 256), BF16), shape((TOK, 1024))],
        tokens,
        mixing_content_matrix,
        own,
        mixing_switch_matrix,
        flops=1_000_000_000,
    )
    alignment_result = call(
        last_kernel,
        shape((ROWS, TOK, 64)),
        logits,
        values,
        gates,
        mixing_final_matrix.T,
        alignment_source,
        alignment_expand_matrix,
        alignment_shrink_matrix.T,
        scratch=[pltpu.VMEM((256, 2048), BF16), pltpu.VMEM((256, 2048), BF16)],
        flops=500_000_000,
    )
    return (alignment_result, couple_result)


def solution(mesh):
    rows, pairs = P("tj", "ti", None), P("ti", "tj", None)
    return jax.shard_map(
        shards,
        mesh=mesh,
        in_specs=(rows, pairs) + (P(),) * 10,
        out_specs=(rows, pairs),
        check_vma=False,
    )
```

```python
import jax
import jax.numpy as jnp
from jax import lax
from jax.experimental import pallas as pl
from jax.experimental.pallas import tpu as pltpu
from jax.sharding import PartitionSpec as P

F32 = jnp.float32
BF16 = jnp.bfloat16
EPS = 1e-05
TI = 8
TJ = 16
ROWS = 4
TOK = 32
COLS = 16
ORDER_TI = [k ^ 6 for k in range(8)]
ORDER_TJ = [k ^ 11 for k in range(16)]
ORDER_LOGITS = [k ^ 10 for k in range(16)]
NN = (((1,), (0,)), ((), ()))
NT = (((1,), (1,)), ((), ()))


def dot(a, b, dims=NN):
    return lax.dot_general(a, b, dims, preferred_element_type=F32)


def split(x):
    hi = x.astype(BF16)
    return hi, (x - hi.astype(F32)).astype(BF16)


def dot3(a, b, dims=NN):
    (ah, al), (bh, bl) = a, b
    return dot(ah, bh, dims) + dot(ah, bl, dims) + dot(al, bh, dims)


def iota(shape, dim):
    return lax.broadcasted_iota(jnp.int32, shape, dim)


def normed(x):
    centred = x - jnp.mean(x, axis=-1, keepdims=True)
    var = jnp.mean(centred * centred, axis=-1, keepdims=True)
    return centred * lax.rsqrt(var + EPS)


def head_tiles(w):
    group = iota((64, 128), 1) // 32
    tiles = []
    for half in range(2):
        part = w[:, half * 128 : half * 128 + 128]
        turned = [pltpu.roll(part, 32 * d, 1) if d else part for d in range(4)]
        for q in range(4):
            tile = turned[(3 - q) % 4]
            for s in range(3):
                tile = jnp.where(group == s, turned[(s - q) % 4], tile)
            tiles.append(tile)
    return tiles


def head_weights(w):
    group = iota((64, 128), 1) // 32
    zero = jnp.zeros((64, 128), BF16)
    out = []
    for tile in head_tiles(w):
        out.append(
            tuple(
                jnp.concatenate([jnp.where(group == s, part, zero) for s in range(ROWS)], axis=0)
                for part in split(tile)
            )
        )
    return out


def first_kernel(x_ref, send_ref, own_ref):
    x = normed(x_ref[...])
    low = jnp.concatenate([x[0], x[1]], axis=1)
    high = jnp.concatenate([x[2], x[3]], axis=1)
    own_ref[:, :128] = low
    own_ref[:, 128:] = high
    for d in range(TI):
        send_ref[d, :TOK, :] = low
        send_ref[d, TOK:, :] = high


def all_tokens(recv_ref):
    slots = [ORDER_TI.index(d) for d in range(TI)]
    return (
        jnp.concatenate([recv_ref[k, :TOK, :] for k in slots], axis=0),
        jnp.concatenate([recv_ref[k, TOK:, :] for k in slots], axis=0),
    )


def factors_kernel(recv_ref, own_ref, w_ref, send_ref):
    w = w_ref[...]
    group = iota((64, 128), 1) // 32
    twice = jnp.concatenate([w, w], axis=1)
    wide = split(jnp.where(group % 2 == 1, twice, pltpu.roll(twice, 96, 1)))
    zero = jnp.zeros((64, 128), BF16)
    wr = [[jnp.where(group == s, part, zero) for s in range(ROWS)] for part in wide]
    low, high = (split(x) for x in all_tokens(recv_ref))
    wr_low = tuple(jnp.concatenate(tiles[:2], axis=0) for tiles in wr)
    wr_high = tuple(jnp.concatenate(tiles[2:], axis=0) for tiles in wr)
    right = dot3(low, wr_low) + dot3(high, wr_high)
    xs = tuple(jnp.concatenate([part] * 4, axis=0) for part in split(own_ref[...]))
    pick = (iota((128, 64), 0) // 4 == iota((128, 64), 1)).astype(BF16)
    keep = iota((128, 256), 0) % 4 == iota((128, 256), 1) // 64
    wl = []
    for part in split(w):
        rows = dot(pick, part, NT)
        wl.append(jnp.where(keep, jnp.concatenate([rows] * 4, axis=1), 0.0).astype(BF16))
    prod = dot3(tuple(wl), xs, NT) * (1.0 / 64.0)
    group = iota((16, 128), 1) // 32
    left = []
    for half in range(2):
        out = jnp.zeros((16, 128), F32)
        for q in range(4):
            at = half * 64 + q * 16
            out = jnp.where(group == q, prod[at : at + 16], out)
        left.append(out)
    for d in range(TJ):
        send_ref[d, :16, :] = left[0]
        send_ref[d, 16:32, :] = left[1]
        at = ORDER_TJ[d] * COLS
        send_ref[d, 32:, :] = right[at : at + COLS]


def values_kernel(recv_ref, wv_ref, own_ref, wg_ref, v_ref, gate_ref):
    own = split(own_ref[...])
    for h, wg in enumerate(head_weights(wg_ref[...])):
        gate_ref[:, h * 128 : h * 128 + 128] = 1.0 / (1.0 + jnp.exp(-dot3(own, wg)))
    low, high = all_tokens(recv_ref)
    xs = split(jnp.concatenate([low, high], axis=1))
    for h, wv in enumerate(head_weights(wv_ref[...])):
        vh, vl = split(dot3(xs, wv))
        for d in range(TJ):
            at, of = (d * 8 + h) * COLS, ORDER_LOGITS[d] * COLS
            v_ref[at : at + COLS, :128] = vh[of : of + COLS]
            v_ref[at : at + COLS, 128:] = vl[of : of + COLS]


def pair_kernel(recv_ref, pair_ref, t_ref, score_ref, mid_ref, send_ref):
    rows = [
        jnp.concatenate([recv_ref[:, r, :], recv_ref[:, 16 + r, :]], axis=1) for r in range(16)
    ]
    left = jnp.concatenate(rows, axis=0).T
    lh, ll = split(left)
    left2 = jnp.concatenate([lh, ll], axis=0)
    group = iota((16, 128), 1) // 32
    zero = jnp.zeros((16, 128), BF16)
    column = iota((TOK, 128), 1) % 16
    tile = jnp.zeros((TOK, 128), F32)
    th, tl = split(t_ref[...])
    fh, fl = [], []
    for pair in range(COLS // 2):
        blocks = []
        for j in (2 * pair, 2 * pair + 1):
            right = recv_ref[:, 32 + j, :]
            turned = [split(pltpu.roll(right, 32 * d, 1) if d else right) for d in range(4)]
            parts = []
            for which in range(2):
                tiles = [
                    jnp.where(group == a, turned[(a - s) % 4][which], zero)
                    for a in range(4)
                    for s in range(4)
                ]
                parts.append(jnp.concatenate(tiles, axis=0))
            blocks.append(parts)
        both = dot(left2, jnp.concatenate([b[0] for b in blocks], axis=1))
        outer = both[:256] + both[256:] + dot(lh, jnp.concatenate([b[1] for b in blocks], axis=1))
        oh, ol = split(outer)
        for q in range(2):
            for part, keep in ((oh, fh), (ol, fl)):
                keep.append(
                    jnp.concatenate(
                        [part[g * 32 : g * 32 + 32, q * 128 : q * 128 + 128] for g in range(8)], axis=1
                    )
                )
    wide = dot(jnp.concatenate(fh + fl, axis=0), jnp.concatenate([th, tl], axis=1))
    update = wide[:512, :128] + wide[:512, 128:] + wide[512:, :128]
    normal = []
    for j in range(COLS):
        mid = pair_ref[:, j, :] + update[j * TOK : (j + 1) * TOK]
        mid_ref[j] = mid
        normal.append(normed(mid))
    nh, nl = split(jnp.concatenate(normal, axis=0))
    score = score_ref[...]
    score = [jnp.broadcast_to(score[h : h + 1], (16, 128)) for h in range(8)]
    logits = dot3((nh, nl), split(jnp.concatenate(score, axis=0)), NT)
    for j in range(COLS):
        tile = jnp.where(column == j, logits[j * TOK : (j + 1) * TOK], tile)
    for d in range(TJ):
        send_ref[d] = tile


def pair_transition_kernel(mid_ref, expand_ref, shrink_ref, out_ref):
    eh, el = split(expand_ref[...])
    expand3 = jnp.concatenate([eh, eh, el], axis=0)
    sh, sl = split(shrink_ref[...])
    shrink2 = jnp.concatenate([sh, sl], axis=1)
    step = 4
    for at in range(0, COLS, step):
        mid = mid_ref[at : at + step].reshape(step * TOK, 128)
        nh, nl = split(normed(mid))
        hidden = dot(jnp.concatenate([nh, nl, nh], axis=1), expand3)
        gate = hidden[:, :512]
        act = gate / (1.0 + jnp.exp(-gate)) * hidden[:, 512:]
        ah, al = split(act)
        wide = dot(ah, shrink2)
        out = mid + wide[:, :128] + wide[:, 128:] + dot(al, sh)
        for j in range(step):
            out_ref[:, at + j, :] = out[j * TOK : (j + 1) * TOK]


def group_all(x, op):
    lane = iota(x.shape, 1)
    for d in (8, 4, 2, 1):
        other = jnp.where((lane & d) == 0, pltpu.roll(x, 128 - d, 1), pltpu.roll(x, d, 1))
        x = op(x, other)
    return x


def three(a, b):
    (ah, al), (bh, bl) = a, b
    return dot(jnp.concatenate([ah, ah, al], axis=1), jnp.concatenate([bh, bl, bh], axis=1), NT)


def swap_groups(tiles):
    group = iota(tiles[0].shape, 1) // 32
    for d in (2, 1):
        low = (group & d) == 0
        out = list(tiles)
        for t in range(4):
            if t & d == 0:
                a, b = tiles[t], tiles[t | d]
                out[t] = jnp.where(low, a, pltpu.roll(b, 32 * d, 1))
                out[t | d] = jnp.where(low, pltpu.roll(a, 128 - 32 * d, 1), b)
        tiles = out
    return tiles


def last_kernel(
    recv_ref, v_ref, gate_ref, wf_ref, x_ref, expand_ref, shrink_ref, out_ref
):
    top = recv_ref[0]
    for d in range(1, TJ):
        top = jnp.maximum(top, recv_ref[d])
    top = group_all(top, jnp.maximum)
    terms = [jnp.exp(recv_ref[d] - top) for d in range(TJ)]
    total = terms[0]
    for d in range(1, TJ):
        total = total + terms[d]
    inv = 1.0 / group_all(total, jnp.add)
    head = iota((TOK, 128), 1) // 16
    zero = jnp.zeros((TOK, 128), BF16)
    high, low = [], []
    for d in range(TJ):
        for part, keep in zip(split(terms[d]), (high, low)):
            keep.append(jnp.concatenate([jnp.where(head == h, part, zero) for h in range(8)], axis=0))
    wide = dot(jnp.concatenate(high, axis=1), v_ref[...])
    mixed = wide[:, :128] + wide[:, 128:] + dot(jnp.concatenate(low, axis=1), v_ref[:, :128])
    gated = [
        mixed[h * TOK : (h + 1) * TOK]
        * (gate_ref[:, h * 128 : h * 128 + 128] * inv[:, h * 16 : h * 16 + 1])
        for h in range(8)
    ]
    halves = [swap_groups(gated[:4]), swap_groups(gated[4:])]
    rows = jnp.concatenate(
        [jnp.concatenate([halves[0][s], halves[1][s]], axis=1) for s in range(ROWS)], axis=0
    )
    mid = x_ref[...].reshape(ROWS * TOK, 64) + three(split(rows), split(wf_ref[...]))
    nh, nl = split(normed(mid))
    eh, el = split(expand_ref[...])
    hidden = dot(jnp.concatenate([nh, nl, nh], axis=1), jnp.concatenate([eh, eh, el], axis=0))
    gate = hidden[:, :256]
    act = gate / (1.0 + jnp.exp(-gate)) * hidden[:, 256:]
    ah, al = split(act)
    sh, sl = split(shrink_ref[...])
    out = mid + dot(
        jnp.concatenate([ah, ah, al], axis=1), jnp.concatenate([sh, sl, sh], axis=1), NT
    )
    out_ref[...] = out.reshape(ROWS, TOK, 64)


def call(kernel, outs, *args, specs=None, scratch=(), flops=0):
    vmem = pl.BlockSpec(memory_space=pltpu.VMEM)
    in_specs = [vmem] * len(args) if specs is None else [s or vmem for s in specs]
    single = not isinstance(outs, (list, tuple))
    outs = [outs] if single else list(outs)
    moved = sum(a.size * a.dtype.itemsize for a in args) + sum(
        o.size * o.dtype.itemsize for o in outs
    )
    res = pl.pallas_call(
        kernel,
        out_shape=outs,
        in_specs=in_specs,
        out_specs=[vmem] * len(outs),
        scratch_shapes=list(scratch),
        compiler_params=pltpu.CompilerParams(vmem_limit_bytes=24 << 20),
        cost_estimate=pl.CostEstimate(flops=flops, bytes_accessed=moved, transcendentals=0),
    )(*args)
    return res[0] if single else res


def shape(dims, dtype=F32):
    return jax.ShapeDtypeStruct(dims, dtype)


def exchange(x, axis, order):
    return lax.all_to_all(x, axis, 0, 0, axis_index_groups=[order], tiled=True)


def shards(
    alignment_source,
    couple_source,
    tensor_operand_matrix,
    tensor_final_matrix,
    mixing_content_matrix,
    mixing_switch_matrix,
    mixing_score_matrix,
    mixing_final_matrix,
    alignment_expand_matrix,
    alignment_shrink_matrix,
    couple_expand_matrix,
    couple_shrink_matrix,
):
    send, own = call(first_kernel, [shape((TI, 64, 128)), shape((TOK, 256))], alignment_source)
    tokens = exchange(send, "ti", ORDER_TI)
    factors = call(factors_kernel, shape((TJ, 48, 128)), tokens, own, tensor_operand_matrix)
    factors = exchange(factors, "tj", ORDER_TJ)
    mid, logits = call(
        pair_kernel,
        [shape((COLS, TOK, 128)), shape((TJ, TOK, 128))],
        factors,
        couple_source,
        tensor_final_matrix,
        mixing_score_matrix.T,
        flops=2_000_000_000,
    )
    mid, tokens = lax.optimization_barrier((mid, tokens))
    logits = exchange(logits, "tj", ORDER_LOGITS)
    couple_result = call(
        pair_transition_kernel,
        shape((TOK, COLS, 128)),
        mid,
        couple_expand_matrix,
        couple_shrink_matrix,
        flops=1_000_000_000,
    )
    values, gates = call(
        values_kernel,
        [shape((2048, 256), BF16), shape((TOK, 1024))],
        tokens,
        mixing_content_matrix,
        own,
        mixing_switch_matrix,
        flops=1_000_000_000,
    )
    alignment_result = call(
        last_kernel,
        shape((ROWS, TOK, 64)),
        logits,
        values,
        gates,
        mixing_final_matrix.T,
        alignment_source,
        alignment_expand_matrix,
        alignment_shrink_matrix.T,
        flops=500_000_000,
    )
    return (alignment_result, couple_result)


def solution(mesh):
    rows, pairs = P("tj", "ti", None), P("ti", "tj", None)
    return jax.shard_map(
        shards,
        mesh=mesh,
        in_specs=(rows, pairs) + (P(),) * 10,
        out_specs=(rows, pairs),
        check_vma=False,
    )
```

```python
import jax
import jax.numpy as jnp
from jax import lax
from jax.experimental import pallas as pl
from jax.experimental.pallas import tpu as pltpu
from jax.sharding import PartitionSpec as P

F32 = jnp.float32
BF16 = jnp.bfloat16
EPS = 1e-05
TI = 8
TJ = 16
ROWS = 4
TOK = 32
COLS = 16
ORDER_TI = [k ^ 6 for k in range(8)]
ORDER_TJ = [k ^ 11 for k in range(16)]
ORDER_LOGITS = [k ^ 10 for k in range(16)]
NN = (((1,), (0,)), ((), ()))
NT = (((1,), (1,)), ((), ()))


def dot(a, b, dims=NN):
    return lax.dot_general(a, b, dims, preferred_element_type=F32)


def split(x):
    hi = x.astype(BF16)
    return hi, (x - hi.astype(F32)).astype(BF16)


def dot3(a, b, dims=NN):
    (ah, al), (bh, bl) = a, b
    return dot(ah, bh, dims) + dot(ah, bl, dims) + dot(al, bh, dims)


def iota(shape, dim):
    return lax.broadcasted_iota(jnp.int32, shape, dim)


def normed(x):
    centred = x - jnp.mean(x, axis=-1, keepdims=True)
    var = jnp.mean(centred * centred, axis=-1, keepdims=True)
    return centred * lax.rsqrt(var + EPS)


def head_tiles(w):
    group = iota((64, 128), 1) // 32
    tiles = []
    for half in range(2):
        part = w[:, half * 128 : half * 128 + 128]
        turned = [pltpu.roll(part, 32 * d, 1) if d else part for d in range(4)]
        for q in range(4):
            tile = turned[(3 - q) % 4]
            for s in range(3):
                tile = jnp.where(group == s, turned[(s - q) % 4], tile)
            tiles.append(tile)
    return tiles


def head_weights(w):
    group = iota((64, 128), 1) // 32
    zero = jnp.zeros((64, 128), BF16)
    out = []
    for tile in head_tiles(w):
        out.append(
            tuple(
                jnp.concatenate([jnp.where(group == s, part, zero) for s in range(ROWS)], axis=0)
                for part in split(tile)
            )
        )
    return out


def first_kernel(x_ref, send_ref, own_ref):
    x = normed(x_ref[...])
    low = jnp.concatenate([x[0], x[1]], axis=1)
    high = jnp.concatenate([x[2], x[3]], axis=1)
    own_ref[:, :128] = low
    own_ref[:, 128:] = high
    for d in range(TI):
        send_ref[d, :TOK, :] = low
        send_ref[d, TOK:, :] = high


def all_tokens(recv_ref):
    slots = [ORDER_TI.index(d) for d in range(TI)]
    return (
        jnp.concatenate([recv_ref[k, :TOK, :] for k in slots], axis=0),
        jnp.concatenate([recv_ref[k, TOK:, :] for k in slots], axis=0),
    )


def factors_kernel(recv_ref, own_ref, w_ref, send_ref):
    w = w_ref[...]
    group = iota((64, 128), 1) // 32
    twice = jnp.concatenate([w, w], axis=1)
    wide = split(jnp.where(group % 2 == 1, twice, pltpu.roll(twice, 96, 1)))
    zero = jnp.zeros((64, 128), BF16)
    wr = [[jnp.where(group == s, part, zero) for s in range(ROWS)] for part in wide]
    low, high = (split(x) for x in all_tokens(recv_ref))
    wr_low = tuple(jnp.concatenate(tiles[:2], axis=0) for tiles in wr)
    wr_high = tuple(jnp.concatenate(tiles[2:], axis=0) for tiles in wr)
    right = dot3(low, wr_low) + dot3(high, wr_high)
    xs = tuple(jnp.concatenate([part] * 4, axis=0) for part in split(own_ref[...]))
    pick = (iota((128, 64), 0) // 4 == iota((128, 64), 1)).astype(BF16)
    keep = iota((128, 256), 0) % 4 == iota((128, 256), 1) // 64
    wl = []
    for part in split(w):
        rows = dot(pick, part, NT)
        wl.append(jnp.where(keep, jnp.concatenate([rows] * 4, axis=1), 0.0).astype(BF16))
    prod = dot3(tuple(wl), xs, NT) * (1.0 / 64.0)
    group = iota((16, 128), 1) // 32
    left = []
    for half in range(2):
        out = jnp.zeros((16, 128), F32)
        for q in range(4):
            at = half * 64 + q * 16
            out = jnp.where(group == q, prod[at : at + 16], out)
        left.append(out)
    for d in range(TJ):
        send_ref[d, :16, :] = left[0]
        send_ref[d, 16:32, :] = left[1]
        at = ORDER_TJ[d] * COLS
        send_ref[d, 32:, :] = right[at : at + COLS]


def values_part(recv_ref, wv_ref, own_ref, wg_ref, v_ref, gate_ref):
    own = split(own_ref[...])
    for h, wg in enumerate(head_weights(wg_ref[...])):
        gate_ref[:, h * 128 : h * 128 + 128] = 1.0 / (1.0 + jnp.exp(-dot3(own, wg)))
    low, high = all_tokens(recv_ref)
    xs = split(jnp.concatenate([low, high], axis=1))
    for h, wv in enumerate(head_weights(wv_ref[...])):
        vh, vl = split(dot3(xs, wv))
        for d in range(TJ):
            at, of = (d * 8 + h) * COLS, ORDER_LOGITS[d] * COLS
            v_ref[at : at + COLS, :128] = vh[of : of + COLS]
            v_ref[at : at + COLS, 128:] = vl[of : of + COLS]


def pair_kernel(recv_ref, pair_ref, t_ref, score_ref, mid_ref, send_ref):
    rows = [
        jnp.concatenate([recv_ref[:, r, :], recv_ref[:, 16 + r, :]], axis=1) for r in range(16)
    ]
    left = jnp.concatenate(rows, axis=0).T
    lh, ll = split(left)
    left2 = jnp.concatenate([lh, ll], axis=0)
    group = iota((16, 128), 1) // 32
    zero = jnp.zeros((16, 128), BF16)
    column = iota((TOK, 128), 1) % 16
    tile = jnp.zeros((TOK, 128), F32)
    th, tl = split(t_ref[...])
    fh, fl = [], []
    for pair in range(COLS // 2):
        blocks = []
        for j in (2 * pair, 2 * pair + 1):
            right = recv_ref[:, 32 + j, :]
            turned = [split(pltpu.roll(right, 32 * d, 1) if d else right) for d in range(4)]
            parts = []
            for which in range(2):
                tiles = [
                    jnp.where(group == a, turned[(a - s) % 4][which], zero)
                    for a in range(4)
                    for s in range(4)
                ]
                parts.append(jnp.concatenate(tiles, axis=0))
            blocks.append(parts)
        both = dot(left2, jnp.concatenate([b[0] for b in blocks], axis=1))
        outer = both[:256] + both[256:] + dot(lh, jnp.concatenate([b[1] for b in blocks], axis=1))
        oh, ol = split(outer)
        for q in range(2):
            for part, keep in ((oh, fh), (ol, fl)):
                keep.append(
                    jnp.concatenate(
                        [part[g * 32 : g * 32 + 32, q * 128 : q * 128 + 128] for g in range(8)], axis=1
                    )
                )
    wide = dot(jnp.concatenate(fh + fl, axis=0), jnp.concatenate([th, tl], axis=1))
    update = wide[:512, :128] + wide[:512, 128:] + wide[512:, :128]
    normal = []
    for j in range(COLS):
        mid = pair_ref[:, j, :] + update[j * TOK : (j + 1) * TOK]
        mid_ref[j] = mid
        normal.append(normed(mid))
    nh, nl = split(jnp.concatenate(normal, axis=0))
    score = score_ref[...]
    score = [jnp.broadcast_to(score[h : h + 1], (16, 128)) for h in range(8)]
    logits = dot3((nh, nl), split(jnp.concatenate(score, axis=0)), NT)
    for j in range(COLS):
        tile = jnp.where(column == j, logits[j * TOK : (j + 1) * TOK], tile)
    for d in range(TJ):
        send_ref[d] = tile


def window_kernel(
    mid_ref, expand_ref, shrink_ref, recv_ref, wv_ref, own_ref, wg_ref,
    result_ref, v_ref, gate_ref, out_ref, sem,
):
    eh, el = split(expand_ref[...])
    expand3 = jnp.concatenate([eh, eh, el], axis=0)
    sh, sl = split(shrink_ref[...])
    shrink2 = jnp.concatenate([sh, sl], axis=1)
    step = 4
    for at in range(0, COLS, step):
        mid = mid_ref[at : at + step].reshape(step * TOK, 128)
        nh, nl = split(normed(mid))
        hidden = dot(jnp.concatenate([nh, nl, nh], axis=1), expand3)
        gate = hidden[:, :512]
        act = gate / (1.0 + jnp.exp(-gate)) * hidden[:, 512:]
        ah, al = split(act)
        wide = dot(ah, shrink2)
        out = mid + wide[:, :128] + wide[:, 128:] + dot(al, sh)
        for j in range(step):
            out_ref[:, at + j, :] = out[j * TOK : (j + 1) * TOK]
    copy = pltpu.make_async_copy(out_ref, result_ref, sem)
    copy.start()
    values_part(recv_ref, wv_ref, own_ref, wg_ref, v_ref, gate_ref)
    copy.wait()


def group_all(x, op):
    lane = iota(x.shape, 1)
    for d in (8, 4, 2, 1):
        other = jnp.where((lane & d) == 0, pltpu.roll(x, 128 - d, 1), pltpu.roll(x, d, 1))
        x = op(x, other)
    return x


def three(a, b):
    (ah, al), (bh, bl) = a, b
    return dot(jnp.concatenate([ah, ah, al], axis=1), jnp.concatenate([bh, bl, bh], axis=1), NT)


def swap_groups(tiles):
    group = iota(tiles[0].shape, 1) // 32
    for d in (2, 1):
        low = (group & d) == 0
        out = list(tiles)
        for t in range(4):
            if t & d == 0:
                a, b = tiles[t], tiles[t | d]
                out[t] = jnp.where(low, a, pltpu.roll(b, 32 * d, 1))
                out[t | d] = jnp.where(low, pltpu.roll(a, 128 - 32 * d, 1), b)
        tiles = out
    return tiles


def last_kernel(
    recv_ref, v_ref, gate_ref, wf_ref, x_ref, expand_ref, shrink_ref, out_ref
):
    top = recv_ref[0]
    for d in range(1, TJ):
        top = jnp.maximum(top, recv_ref[d])
    top = group_all(top, jnp.maximum)
    terms = [jnp.exp(recv_ref[d] - top) for d in range(TJ)]
    total = terms[0]
    for d in range(1, TJ):
        total = total + terms[d]
    inv = 1.0 / group_all(total, jnp.add)
    head = iota((TOK, 128), 1) // 16
    zero = jnp.zeros((TOK, 128), BF16)
    high, low = [], []
    for d in range(TJ):
        for part, keep in zip(split(terms[d]), (high, low)):
            keep.append(jnp.concatenate([jnp.where(head == h, part, zero) for h in range(8)], axis=0))
    wide = dot(jnp.concatenate(high, axis=1), v_ref[...])
    mixed = wide[:, :128] + wide[:, 128:] + dot(jnp.concatenate(low, axis=1), v_ref[:, :128])
    gated = [
        mixed[h * TOK : (h + 1) * TOK]
        * (gate_ref[:, h * 128 : h * 128 + 128] * inv[:, h * 16 : h * 16 + 1])
        for h in range(8)
    ]
    halves = [swap_groups(gated[:4]), swap_groups(gated[4:])]
    rows = jnp.concatenate(
        [jnp.concatenate([halves[0][s], halves[1][s]], axis=1) for s in range(ROWS)], axis=0
    )
    mid = x_ref[...].reshape(ROWS * TOK, 64) + three(split(rows), split(wf_ref[...]))
    nh, nl = split(normed(mid))
    eh, el = split(expand_ref[...])
    hidden = dot(jnp.concatenate([nh, nl, nh], axis=1), jnp.concatenate([eh, eh, el], axis=0))
    gate = hidden[:, :256]
    act = gate / (1.0 + jnp.exp(-gate)) * hidden[:, 256:]
    ah, al = split(act)
    sh, sl = split(shrink_ref[...])
    out = mid + dot(
        jnp.concatenate([ah, ah, al], axis=1), jnp.concatenate([sh, sl, sh], axis=1), NT
    )
    out_ref[...] = out.reshape(ROWS, TOK, 64)


def call(kernel, outs, *args, out_specs=None, specs=None, scratch=(), flops=0):
    vmem = pl.BlockSpec(memory_space=pltpu.VMEM)
    in_specs = [vmem] * len(args) if specs is None else [s or vmem for s in specs]
    single = not isinstance(outs, (list, tuple))
    outs = [outs] if single else list(outs)
    moved = sum(a.size * a.dtype.itemsize for a in args) + sum(
        o.size * o.dtype.itemsize for o in outs
    )
    res = pl.pallas_call(
        kernel,
        out_shape=outs,
        in_specs=in_specs,
        out_specs=[vmem] * len(outs) if out_specs is None else [o or vmem for o in out_specs],
        scratch_shapes=list(scratch),
        compiler_params=pltpu.CompilerParams(vmem_limit_bytes=24 << 20),
        cost_estimate=pl.CostEstimate(flops=flops, bytes_accessed=moved, transcendentals=0),
    )(*args)
    return res[0] if single else res


def shape(dims, dtype=F32):
    return jax.ShapeDtypeStruct(dims, dtype)


def exchange(x, axis, order):
    return lax.all_to_all(x, axis, 0, 0, axis_index_groups=[order], tiled=True)


def shards(
    alignment_source,
    couple_source,
    tensor_operand_matrix,
    tensor_final_matrix,
    mixing_content_matrix,
    mixing_switch_matrix,
    mixing_score_matrix,
    mixing_final_matrix,
    alignment_expand_matrix,
    alignment_shrink_matrix,
    couple_expand_matrix,
    couple_shrink_matrix,
):
    send, own = call(first_kernel, [shape((TI, 64, 128)), shape((TOK, 256))], alignment_source)
    tokens = exchange(send, "ti", ORDER_TI)
    factors = call(factors_kernel, shape((TJ, 48, 128)), tokens, own, tensor_operand_matrix)
    factors = exchange(factors, "tj", ORDER_TJ)
    mid, logits = call(
        pair_kernel,
        [shape((COLS, TOK, 128)), shape((TJ, TOK, 128))],
        factors,
        couple_source,
        tensor_final_matrix,
        mixing_score_matrix.T,
        flops=2_000_000_000,
    )
    mid, tokens = lax.optimization_barrier((mid, tokens))
    logits = exchange(logits, "tj", ORDER_LOGITS)
    couple_result, values, gates = call(
        window_kernel,
        [shape((TOK, COLS, 128)), shape((2048, 256), BF16), shape((TOK, 1024))],
        mid,
        couple_expand_matrix,
        couple_shrink_matrix,
        tokens,
        mixing_content_matrix,
        own,
        mixing_switch_matrix,
        out_specs=[pl.BlockSpec(memory_space=pl.ANY), None, None],
        scratch=[pltpu.VMEM((TOK, COLS, 128), F32), pltpu.SemaphoreType.DMA(())],
        flops=2_000_000_000,
    )
    alignment_result = call(
        last_kernel,
        shape((ROWS, TOK, 64)),
        logits,
        values,
        gates,
        mixing_final_matrix.T,
        alignment_source,
        alignment_expand_matrix,
        alignment_shrink_matrix.T,
        flops=500_000_000,
    )
    return (alignment_result, couple_result)


def solution(mesh):
    rows, pairs = P("tj", "ti", None), P("ti", "tj", None)
    return jax.shard_map(
        shards,
        mesh=mesh,
        in_specs=(rows, pairs) + (P(),) * 10,
        out_specs=(rows, pairs),
        check_vma=False,
    )
```

```python
import jax
import jax.numpy as jnp
from jax import lax
from jax.experimental import pallas as pl
from jax.experimental.pallas import tpu as pltpu
from jax.sharding import PartitionSpec as P

F32 = jnp.float32
BF16 = jnp.bfloat16
EPS = 1e-05
TI = 8
TJ = 16
ROWS = 4
TOK = 32
COLS = 16
ORDER_TI = [k ^ 6 for k in range(8)]
ORDER_TJ = [k ^ 11 for k in range(16)]
ORDER_LOGITS = [k ^ 10 for k in range(16)]
NN = (((1,), (0,)), ((), ()))
NT = (((1,), (1,)), ((), ()))


def dot(a, b, dims=NN):
    return lax.dot_general(a, b, dims, preferred_element_type=F32)


def split(x):
    hi = x.astype(BF16)
    return hi, (x - hi.astype(F32)).astype(BF16)


def dot3(a, b, dims=NN):
    (ah, al), (bh, bl) = a, b
    return dot(ah, bh, dims) + dot(ah, bl, dims) + dot(al, bh, dims)


def iota(shape, dim):
    return lax.broadcasted_iota(jnp.int32, shape, dim)


def normed(x):
    centred = x - jnp.mean(x, axis=-1, keepdims=True)
    var = jnp.mean(centred * centred, axis=-1, keepdims=True)
    return centred * lax.rsqrt(var + EPS)


def head_tiles(w):
    group = iota((64, 128), 1) // 32
    tiles = []
    for half in range(2):
        part = w[:, half * 128 : half * 128 + 128]
        turned = [pltpu.roll(part, 32 * d, 1) if d else part for d in range(4)]
        for q in range(4):
            tile = turned[(3 - q) % 4]
            for s in range(3):
                tile = jnp.where(group == s, turned[(s - q) % 4], tile)
            tiles.append(tile)
    return tiles


def head_weights(w):
    group = iota((64, 128), 1) // 32
    zero = jnp.zeros((64, 128), BF16)
    out = []
    for tile in head_tiles(w):
        out.append(
            tuple(
                jnp.concatenate([jnp.where(group == s, part, zero) for s in range(ROWS)], axis=0)
                for part in split(tile)
            )
        )
    return out


def first_kernel(x_ref, send_ref):
    x = normed(x_ref[...])
    low = jnp.concatenate([x[0], x[1]], axis=1)
    high = jnp.concatenate([x[2], x[3]], axis=1)
    for d in range(TI):
        send_ref[d, :TOK, :] = low
        send_ref[d, TOK:, :] = high


def all_tokens(recv_ref):
    slots = [ORDER_TI.index(d) for d in range(TI)]
    return (
        jnp.concatenate([recv_ref[k, :TOK, :] for k in slots], axis=0),
        jnp.concatenate([recv_ref[k, TOK:, :] for k in slots], axis=0),
    )


def factors_kernel(recv_ref, own_ref, w_ref, send_ref):
    w = w_ref[...]
    group = iota((64, 128), 1) // 32
    twice = jnp.concatenate([w, w], axis=1)
    wide = split(jnp.where(group % 2 == 1, twice, pltpu.roll(twice, 96, 1)))
    zero = jnp.zeros((64, 128), BF16)
    wr = [[jnp.where(group == s, part, zero) for s in range(ROWS)] for part in wide]
    low, high = (split(x) for x in all_tokens(recv_ref))
    wr_low = tuple(jnp.concatenate(tiles[:2], axis=0) for tiles in wr)
    wr_high = tuple(jnp.concatenate(tiles[2:], axis=0) for tiles in wr)
    right = dot3(low, wr_low) + dot3(high, wr_high)
    xs = tuple(jnp.concatenate([part] * 4, axis=0) for part in split(jnp.concatenate([own_ref[0, :TOK, :], own_ref[0, TOK:, :]], axis=1)))
    pick = (iota((128, 64), 0) // 4 == iota((128, 64), 1)).astype(BF16)
    keep = iota((128, 256), 0) % 4 == iota((128, 256), 1) // 64
    wl = []
    for part in split(w):
        rows = dot(pick, part, NT)
        wl.append(jnp.where(keep, jnp.concatenate([rows] * 4, axis=1), 0.0).astype(BF16))
    prod = dot3(tuple(wl), xs, NT) * (1.0 / 64.0)
    group = iota((16, 128), 1) // 32
    left = []
    for half in range(2):
        out = jnp.zeros((16, 128), F32)
        for q in range(4):
            at = half * 64 + q * 16
            out = jnp.where(group == q, prod[at : at + 16], out)
        left.append(out)
    for d in range(TJ):
        send_ref[d, :16, :] = left[0]
        send_ref[d, 16:32, :] = left[1]
        at = ORDER_TJ[d] * COLS
        send_ref[d, 32:, :] = right[at : at + COLS]


def values_part(recv_ref, wv_ref, own_ref, wg_ref, v_ref, gate_ref):
    own = split(jnp.concatenate([own_ref[0, :TOK, :], own_ref[0, TOK:, :]], axis=1))
    for h, wg in enumerate(head_weights(wg_ref[...])):
        gate_ref[:, h * 128 : h * 128 + 128] = 1.0 / (1.0 + jnp.exp(-dot3(own, wg)))
    low, high = all_tokens(recv_ref)
    xs = split(jnp.concatenate([low, high], axis=1))
    for h, wv in enumerate(head_weights(wv_ref[...])):
        vh, vl = split(dot3(xs, wv))
        for d in range(TJ):
            at, of = (d * 8 + h) * COLS, ORDER_LOGITS[d] * COLS
            v_ref[at : at + COLS, :128] = vh[of : of + COLS]
            v_ref[at : at + COLS, 128:] = vl[of : of + COLS]


def pair_kernel(recv_ref, pair_ref, t_ref, score_ref, mid_ref, send_ref):
    rows = [
        jnp.concatenate([recv_ref[:, r, :], recv_ref[:, 16 + r, :]], axis=1) for r in range(16)
    ]
    left = jnp.concatenate(rows, axis=0).T
    lh, ll = split(left)
    left2 = jnp.concatenate([lh, ll], axis=0)
    group = iota((16, 128), 1) // 32
    zero = jnp.zeros((16, 128), BF16)
    column = iota((TOK, 128), 1) % 16
    tile = jnp.zeros((TOK, 128), F32)
    th, tl = split(t_ref[...])
    fh, fl = [], []
    for pair in range(COLS // 2):
        blocks = []
        for j in (2 * pair, 2 * pair + 1):
            right = recv_ref[:, 32 + j, :]
            turned = [split(pltpu.roll(right, 32 * d, 1) if d else right) for d in range(4)]
            parts = []
            for which in range(2):
                tiles = [
                    jnp.where(group == a, turned[(a - s) % 4][which], zero)
                    for a in range(4)
                    for s in range(4)
                ]
                parts.append(jnp.concatenate(tiles, axis=0))
            blocks.append(parts)
        both = dot(left2, jnp.concatenate([b[0] for b in blocks], axis=1))
        outer = both[:256] + both[256:] + dot(lh, jnp.concatenate([b[1] for b in blocks], axis=1))
        oh, ol = split(outer)
        for q in range(2):
            for part, keep in ((oh, fh), (ol, fl)):
                keep.append(
                    jnp.concatenate(
                        [part[g * 32 : g * 32 + 32, q * 128 : q * 128 + 128] for g in range(8)], axis=1
                    )
                )
    wide = dot(jnp.concatenate(fh + fl, axis=0), jnp.concatenate([th, tl], axis=1))
    update = wide[:512, :128] + wide[:512, 128:] + wide[512:, :128]
    normal = []
    for j in range(COLS):
        mid = pair_ref[:, j, :] + update[j * TOK : (j + 1) * TOK]
        mid_ref[j] = mid
        normal.append(normed(mid))
    nh, nl = split(jnp.concatenate(normal, axis=0))
    score = score_ref[...]
    score = [jnp.broadcast_to(score[h : h + 1], (16, 128)) for h in range(8)]
    logits = dot3((nh, nl), split(jnp.concatenate(score, axis=0)), NT)
    for j in range(COLS):
        tile = jnp.where(column == j, logits[j * TOK : (j + 1) * TOK], tile)
    for d in range(TJ):
        send_ref[d] = tile


def window_kernel(
    mid_ref, expand_ref, shrink_ref, recv_ref, wv_ref, own_ref, wg_ref,
    result_ref, v_ref, gate_ref, out_ref, sem,
):
    eh, el = split(expand_ref[...])
    expand3 = jnp.concatenate([eh, eh, el], axis=0)
    sh, sl = split(shrink_ref[...])
    shrink2 = jnp.concatenate([sh, sl], axis=1)
    step = 4
    for at in range(0, COLS, step):
        mid = mid_ref[at : at + step].reshape(step * TOK, 128)
        nh, nl = split(normed(mid))
        hidden = dot(jnp.concatenate([nh, nl, nh], axis=1), expand3)
        gate = hidden[:, :512]
        act = gate / (1.0 + jnp.exp(-gate)) * hidden[:, 512:]
        ah, al = split(act)
        wide = dot(ah, shrink2)
        out = mid + wide[:, :128] + wide[:, 128:] + dot(al, sh)
        for j in range(step):
            out_ref[:, at + j, :] = out[j * TOK : (j + 1) * TOK]
    copy = pltpu.make_async_copy(out_ref, result_ref, sem)
    copy.start()
    values_part(recv_ref, wv_ref, own_ref, wg_ref, v_ref, gate_ref)
    copy.wait()


def group_all(x, op):
    lane = iota(x.shape, 1)
    for d in (8, 4, 2, 1):
        other = jnp.where((lane & d) == 0, pltpu.roll(x, 128 - d, 1), pltpu.roll(x, d, 1))
        x = op(x, other)
    return x


def three(a, b):
    (ah, al), (bh, bl) = a, b
    return dot(jnp.concatenate([ah, ah, al], axis=1), jnp.concatenate([bh, bl, bh], axis=1), NT)


def swap_groups(tiles):
    group = iota(tiles[0].shape, 1) // 32
    for d in (2, 1):
        low = (group & d) == 0
        out = list(tiles)
        for t in range(4):
            if t & d == 0:
                a, b = tiles[t], tiles[t | d]
                out[t] = jnp.where(low, a, pltpu.roll(b, 32 * d, 1))
                out[t | d] = jnp.where(low, pltpu.roll(a, 128 - 32 * d, 1), b)
        tiles = out
    return tiles


def last_kernel(
    recv_ref, v_ref, gate_ref, wf_ref, x_ref, expand_ref, shrink_ref, out_ref
):
    top = recv_ref[0]
    for d in range(1, TJ):
        top = jnp.maximum(top, recv_ref[d])
    top = group_all(top, jnp.maximum)
    terms = [jnp.exp(recv_ref[d] - top) for d in range(TJ)]
    total = terms[0]
    for d in range(1, TJ):
        total = total + terms[d]
    inv = 1.0 / group_all(total, jnp.add)
    head = iota((TOK, 128), 1) // 16
    zero = jnp.zeros((TOK, 128), BF16)
    high, low = [], []
    for d in range(TJ):
        for part, keep in zip(split(terms[d]), (high, low)):
            keep.append(jnp.concatenate([jnp.where(head == h, part, zero) for h in range(8)], axis=0))
    wide = dot(jnp.concatenate(high, axis=1), v_ref[...])
    mixed = wide[:, :128] + wide[:, 128:] + dot(jnp.concatenate(low, axis=1), v_ref[:, :128])
    gated = [
        mixed[h * TOK : (h + 1) * TOK]
        * (gate_ref[:, h * 128 : h * 128 + 128] * inv[:, h * 16 : h * 16 + 1])
        for h in range(8)
    ]
    halves = [swap_groups(gated[:4]), swap_groups(gated[4:])]
    rows = jnp.concatenate(
        [jnp.concatenate([halves[0][s], halves[1][s]], axis=1) for s in range(ROWS)], axis=0
    )
    mid = x_ref[...].reshape(ROWS * TOK, 64) + three(split(rows), split(wf_ref[...]))
    nh, nl = split(normed(mid))
    eh, el = split(expand_ref[...])
    hidden = dot(jnp.concatenate([nh, nl, nh], axis=1), jnp.concatenate([eh, eh, el], axis=0))
    gate = hidden[:, :256]
    act = gate / (1.0 + jnp.exp(-gate)) * hidden[:, 256:]
    ah, al = split(act)
    sh, sl = split(shrink_ref[...])
    out = mid + dot(
        jnp.concatenate([ah, ah, al], axis=1), jnp.concatenate([sh, sl, sh], axis=1), NT
    )
    out_ref[...] = out.reshape(ROWS, TOK, 64)


def call(kernel, outs, *args, out_specs=None, specs=None, scratch=(), flops=0):
    vmem = pl.BlockSpec(memory_space=pltpu.VMEM)
    in_specs = [vmem] * len(args) if specs is None else [s or vmem for s in specs]
    single = not isinstance(outs, (list, tuple))
    outs = [outs] if single else list(outs)
    moved = sum(a.size * a.dtype.itemsize for a in args) + sum(
        o.size * o.dtype.itemsize for o in outs
    )
    res = pl.pallas_call(
        kernel,
        out_shape=outs,
        in_specs=in_specs,
        out_specs=[vmem] * len(outs) if out_specs is None else [o or vmem for o in out_specs],
        scratch_shapes=list(scratch),
        compiler_params=pltpu.CompilerParams(vmem_limit_bytes=24 << 20),
        cost_estimate=pl.CostEstimate(flops=flops, bytes_accessed=moved, transcendentals=0),
    )(*args)
    return res[0] if single else res


def shape(dims, dtype=F32):
    return jax.ShapeDtypeStruct(dims, dtype)


def exchange(x, axis, order):
    return lax.all_to_all(x, axis, 0, 0, axis_index_groups=[order], tiled=True)


def shards(
    alignment_source,
    couple_source,
    tensor_operand_matrix,
    tensor_final_matrix,
    mixing_content_matrix,
    mixing_switch_matrix,
    mixing_score_matrix,
    mixing_final_matrix,
    alignment_expand_matrix,
    alignment_shrink_matrix,
    couple_expand_matrix,
    couple_shrink_matrix,
):
    own = call(first_kernel, shape((TI, 64, 128)), alignment_source)
    tokens = exchange(own, "ti", ORDER_TI)
    factors = call(factors_kernel, shape((TJ, 48, 128)), tokens, own, tensor_operand_matrix)
    factors = exchange(factors, "tj", ORDER_TJ)
    mid, logits = call(
        pair_kernel,
        [shape((COLS, TOK, 128)), shape((TJ, TOK, 128))],
        factors,
        couple_source,
        tensor_final_matrix,
        mixing_score_matrix.T,
        flops=2_000_000_000,
    )
    mid, tokens = lax.optimization_barrier((mid, tokens))
    logits = exchange(logits, "tj", ORDER_LOGITS)
    couple_result, values, gates = call(
        window_kernel,
        [shape((TOK, COLS, 128)), shape((2048, 256), BF16), shape((TOK, 1024))],
        mid,
        couple_expand_matrix,
        couple_shrink_matrix,
        tokens,
        mixing_content_matrix,
        own,
        mixing_switch_matrix,
        out_specs=[pl.BlockSpec(memory_space=pl.ANY), None, None],
        scratch=[pltpu.VMEM((TOK, COLS, 128), F32), pltpu.SemaphoreType.DMA(())],
        flops=2_000_000_000,
    )
    alignment_result = call(
        last_kernel,
        shape((ROWS, TOK, 64)),
        logits,
        values,
        gates,
        mixing_final_matrix.T,
        alignment_source,
        alignment_expand_matrix,
        alignment_shrink_matrix.T,
        flops=500_000_000,
    )
    return (alignment_result, couple_result)


def solution(mesh):
    rows, pairs = P("tj", "ti", None), P("ti", "tj", None)
    return jax.shard_map(
        shards,
        mesh=mesh,
        in_specs=(rows, pairs) + (P(),) * 10,
        out_specs=(rows, pairs),
        check_vma=False,
    )
```

```python
import jax
import jax.numpy as jnp
from jax import lax
from jax.experimental import pallas as pl
from jax.experimental.pallas import tpu as pltpu
from jax.sharding import PartitionSpec as P

F32 = jnp.float32
BF16 = jnp.bfloat16
EPS = 1e-05
TI = 8
TJ = 16
ROWS = 4
TOK = 32
COLS = 16
ORDER_TI = [k ^ 6 for k in range(8)]
ORDER_TJ = [11, 10, 9, 8, 15, 14, 13, 12, 3, 2, 1, 0, 7, 5, 6, 4]
ORDER_LOGITS = [10, 11, 8, 9, 14, 15, 12, 13, 3, 2, 0, 1, 6, 7, 4, 5]
NN = (((1,), (0,)), ((), ()))
NT = (((1,), (1,)), ((), ()))


def dot(a, b, dims=NN):
    return lax.dot_general(a, b, dims, preferred_element_type=F32)


def split(x):
    hi = x.astype(BF16)
    return hi, (x - hi.astype(F32)).astype(BF16)


def dot3(a, b, dims=NN):
    (ah, al), (bh, bl) = a, b
    return dot(ah, bh, dims) + dot(ah, bl, dims) + dot(al, bh, dims)


def iota(shape, dim):
    return lax.broadcasted_iota(jnp.int32, shape, dim)


def normed(x):
    centred = x - jnp.mean(x, axis=-1, keepdims=True)
    var = jnp.mean(centred * centred, axis=-1, keepdims=True)
    return centred * lax.rsqrt(var + EPS)


def head_tiles(w):
    group = iota((64, 128), 1) // 32
    tiles = []
    for half in range(2):
        part = w[:, half * 128 : half * 128 + 128]
        turned = [pltpu.roll(part, 32 * d, 1) if d else part for d in range(4)]
        for q in range(4):
            tile = turned[(3 - q) % 4]
            for s in range(3):
                tile = jnp.where(group == s, turned[(s - q) % 4], tile)
            tiles.append(tile)
    return tiles


def head_weights(w):
    group = iota((64, 128), 1) // 32
    zero = jnp.zeros((64, 128), BF16)
    out = []
    for tile in head_tiles(w):
        out.append(
            tuple(
                jnp.concatenate([jnp.where(group == s, part, zero) for s in range(ROWS)], axis=0)
                for part in split(tile)
            )
        )
    return out


def first_kernel(x_ref, send_ref, own_ref):
    x = normed(x_ref[...])
    low = jnp.concatenate([x[0], x[1]], axis=1)
    high = jnp.concatenate([x[2], x[3]], axis=1)
    own_ref[:, :128] = low
    own_ref[:, 128:] = high
    for d in range(TI):
        send_ref[d, :TOK, :] = low
        send_ref[d, TOK:, :] = high


def all_tokens(recv_ref):
    slots = [ORDER_TI.index(d) for d in range(TI)]
    return (
        jnp.concatenate([recv_ref[k, :TOK, :] for k in slots], axis=0),
        jnp.concatenate([recv_ref[k, TOK:, :] for k in slots], axis=0),
    )


def factors_kernel(recv_ref, own_ref, w_ref, send_ref):
    w = w_ref[...]
    group = iota((64, 128), 1) // 32
    twice = jnp.concatenate([w, w], axis=1)
    wide = split(jnp.where(group % 2 == 1, twice, pltpu.roll(twice, 96, 1)))
    zero = jnp.zeros((64, 128), BF16)
    wr = [[jnp.where(group == s, part, zero) for s in range(ROWS)] for part in wide]
    low, high = (split(x) for x in all_tokens(recv_ref))
    wr_low = tuple(jnp.concatenate(tiles[:2], axis=0) for tiles in wr)
    wr_high = tuple(jnp.concatenate(tiles[2:], axis=0) for tiles in wr)
    right = dot3(low, wr_low) + dot3(high, wr_high)
    xs = tuple(jnp.concatenate([part] * 4, axis=0) for part in split(own_ref[...]))
    pick = (iota((128, 64), 0) // 4 == iota((128, 64), 1)).astype(BF16)
    keep = iota((128, 256), 0) % 4 == iota((128, 256), 1) // 64
    wl = []
    for part in split(w):
        rows = dot(pick, part, NT)
        wl.append(jnp.where(keep, jnp.concatenate([rows] * 4, axis=1), 0.0).astype(BF16))
    prod = dot3(tuple(wl), xs, NT) * (1.0 / 64.0)
    group = iota((16, 128), 1) // 32
    left = []
    for half in range(2):
        out = jnp.zeros((16, 128), F32)
        for q in range(4):
            at = half * 64 + q * 16
            out = jnp.where(group == q, prod[at : at + 16], out)
        left.append(out)
    for d in range(TJ):
        send_ref[d, :16, :] = left[0]
        send_ref[d, 16:32, :] = left[1]
        at = ORDER_TJ[d] * COLS
        send_ref[d, 32:, :] = right[at : at + COLS]


def values_part(recv_ref, wv_ref, own_ref, wg_ref, v_ref, gate_ref):
    own = split(own_ref[...])
    for h, wg in enumerate(head_weights(wg_ref[...])):
        gate_ref[:, h * 128 : h * 128 + 128] = 1.0 / (1.0 + jnp.exp(-dot3(own, wg)))
    low, high = all_tokens(recv_ref)
    xs = split(jnp.concatenate([low, high], axis=1))
    for h, wv in enumerate(head_weights(wv_ref[...])):
        vh, vl = split(dot3(xs, wv))
        for d in range(TJ):
            at, of = (d * 8 + h) * COLS, ORDER_LOGITS[d] * COLS
            v_ref[at : at + COLS, :128] = vh[of : of + COLS]
            v_ref[at : at + COLS, 128:] = vl[of : of + COLS]


def pair_kernel(recv_ref, pair_ref, t_ref, score_ref, mid_ref, send_ref):
    rows = [
        jnp.concatenate([recv_ref[:, r, :], recv_ref[:, 16 + r, :]], axis=1) for r in range(16)
    ]
    left = jnp.concatenate(rows, axis=0).T
    lh, ll = split(left)
    left2 = jnp.concatenate([lh, ll], axis=0)
    group = iota((16, 128), 1) // 32
    zero = jnp.zeros((16, 128), BF16)
    column = iota((TOK, 128), 1) % 16
    tile = jnp.zeros((TOK, 128), F32)
    th, tl = split(t_ref[...])
    fh, fl = [], []
    for pair in range(COLS // 2):
        blocks = []
        for j in (2 * pair, 2 * pair + 1):
            right = recv_ref[:, 32 + j, :]
            turned = [split(pltpu.roll(right, 32 * d, 1) if d else right) for d in range(4)]
            parts = []
            for which in range(2):
                tiles = [
                    jnp.where(group == a, turned[(a - s) % 4][which], zero)
                    for a in range(4)
                    for s in range(4)
                ]
                parts.append(jnp.concatenate(tiles, axis=0))
            blocks.append(parts)
        both = dot(left2, jnp.concatenate([b[0] for b in blocks], axis=1))
        outer = both[:256] + both[256:] + dot(lh, jnp.concatenate([b[1] for b in blocks], axis=1))
        oh, ol = split(outer)
        for q in range(2):
            for part, keep in ((oh, fh), (ol, fl)):
                keep.append(
                    jnp.concatenate(
                        [part[g * 32 : g * 32 + 32, q * 128 : q * 128 + 128] for g in range(8)], axis=1
                    )
                )
    wide = dot(jnp.concatenate(fh + fl, axis=0), jnp.concatenate([th, tl], axis=1))
    update = wide[:512, :128] + wide[:512, 128:] + wide[512:, :128]
    normal = []
    for j in range(COLS):
        mid = pair_ref[:, j, :] + update[j * TOK : (j + 1) * TOK]
        mid_ref[j] = mid
        normal.append(normed(mid))
    nh, nl = split(jnp.concatenate(normal, axis=0))
    score = score_ref[...]
    score = [jnp.broadcast_to(score[h : h + 1], (16, 128)) for h in range(8)]
    logits = dot3((nh, nl), split(jnp.concatenate(score, axis=0)), NT)
    for j in range(COLS):
        tile = jnp.where(column == j, logits[j * TOK : (j + 1) * TOK], tile)
    for d in range(TJ):
        send_ref[d] = tile


def window_kernel(
    mid_ref, expand_ref, shrink_ref, recv_ref, wv_ref, own_ref, wg_ref,
    result_ref, v_ref, gate_ref, out_ref, sem,
):
    eh, el = split(expand_ref[...])
    expand3 = jnp.concatenate([eh, eh, el], axis=0)
    sh, sl = split(shrink_ref[...])
    shrink2 = jnp.concatenate([sh, sl], axis=1)
    step = 4
    for at in range(0, COLS, step):
        mid = mid_ref[at : at + step].reshape(step * TOK, 128)
        nh, nl = split(normed(mid))
        hidden = dot(jnp.concatenate([nh, nl, nh], axis=1), expand3)
        gate = hidden[:, :512]
        act = gate / (1.0 + jnp.exp(-gate)) * hidden[:, 512:]
        ah, al = split(act)
        wide = dot(ah, shrink2)
        out = mid + wide[:, :128] + wide[:, 128:] + dot(al, sh)
        for j in range(step):
            out_ref[:, at + j, :] = out[j * TOK : (j + 1) * TOK]
    copy = pltpu.make_async_copy(out_ref, result_ref, sem)
    copy.start()
    values_part(recv_ref, wv_ref, own_ref, wg_ref, v_ref, gate_ref)
    copy.wait()


def group_all(x, op):
    lane = iota(x.shape, 1)
    for d in (8, 4, 2, 1):
        other = jnp.where((lane & d) == 0, pltpu.roll(x, 128 - d, 1), pltpu.roll(x, d, 1))
        x = op(x, other)
    return x


def three(a, b):
    (ah, al), (bh, bl) = a, b
    return dot(jnp.concatenate([ah, ah, al], axis=1), jnp.concatenate([bh, bl, bh], axis=1), NT)


def swap_groups(tiles):
    group = iota(tiles[0].shape, 1) // 32
    for d in (2, 1):
        low = (group & d) == 0
        out = list(tiles)
        for t in range(4):
            if t & d == 0:
                a, b = tiles[t], tiles[t | d]
                out[t] = jnp.where(low, a, pltpu.roll(b, 32 * d, 1))
                out[t | d] = jnp.where(low, pltpu.roll(a, 128 - 32 * d, 1), b)
        tiles = out
    return tiles


def last_kernel(
    recv_ref, v_ref, gate_ref, wf_ref, x_ref, expand_ref, shrink_ref, out_ref
):
    top = recv_ref[0]
    for d in range(1, TJ):
        top = jnp.maximum(top, recv_ref[d])
    top = group_all(top, jnp.maximum)
    terms = [jnp.exp(recv_ref[d] - top) for d in range(TJ)]
    total = terms[0]
    for d in range(1, TJ):
        total = total + terms[d]
    inv = 1.0 / group_all(total, jnp.add)
    head = iota((TOK, 128), 1) // 16
    zero = jnp.zeros((TOK, 128), BF16)
    high, low = [], []
    for d in range(TJ):
        for part, keep in zip(split(terms[d]), (high, low)):
            keep.append(jnp.concatenate([jnp.where(head == h, part, zero) for h in range(8)], axis=0))
    wide = dot(jnp.concatenate(high, axis=1), v_ref[...])
    mixed = wide[:, :128] + wide[:, 128:] + dot(jnp.concatenate(low, axis=1), v_ref[:, :128])
    gated = [
        mixed[h * TOK : (h + 1) * TOK]
        * (gate_ref[:, h * 128 : h * 128 + 128] * inv[:, h * 16 : h * 16 + 1])
        for h in range(8)
    ]
    halves = [swap_groups(gated[:4]), swap_groups(gated[4:])]
    rows = jnp.concatenate(
        [jnp.concatenate([halves[0][s], halves[1][s]], axis=1) for s in range(ROWS)], axis=0
    )
    mid = x_ref[...].reshape(ROWS * TOK, 64) + three(split(rows), split(wf_ref[...]))
    nh, nl = split(normed(mid))
    eh, el = split(expand_ref[...])
    hidden = dot(jnp.concatenate([nh, nl, nh], axis=1), jnp.concatenate([eh, eh, el], axis=0))
    gate = hidden[:, :256]
    act = gate / (1.0 + jnp.exp(-gate)) * hidden[:, 256:]
    ah, al = split(act)
    sh, sl = split(shrink_ref[...])
    out = mid + dot(
        jnp.concatenate([ah, ah, al], axis=1), jnp.concatenate([sh, sl, sh], axis=1), NT
    )
    out_ref[...] = out.reshape(ROWS, TOK, 64)


def call(kernel, outs, *args, out_specs=None, specs=None, scratch=(), flops=0):
    vmem = pl.BlockSpec(memory_space=pltpu.VMEM)
    in_specs = [vmem] * len(args) if specs is None else [s or vmem for s in specs]
    single = not isinstance(outs, (list, tuple))
    outs = [outs] if single else list(outs)
    moved = sum(a.size * a.dtype.itemsize for a in args) + sum(
        o.size * o.dtype.itemsize for o in outs
    )
    res = pl.pallas_call(
        kernel,
        out_shape=outs,
        in_specs=in_specs,
        out_specs=[vmem] * len(outs) if out_specs is None else [o or vmem for o in out_specs],
        scratch_shapes=list(scratch),
        compiler_params=pltpu.CompilerParams(vmem_limit_bytes=24 << 20),
        cost_estimate=pl.CostEstimate(flops=flops, bytes_accessed=moved, transcendentals=0),
    )(*args)
    return res[0] if single else res


def shape(dims, dtype=F32):
    return jax.ShapeDtypeStruct(dims, dtype)


def exchange(x, axis, order):
    return lax.all_to_all(x, axis, 0, 0, axis_index_groups=[order], tiled=True)


def shards(
    alignment_source,
    couple_source,
    tensor_operand_matrix,
    tensor_final_matrix,
    mixing_content_matrix,
    mixing_switch_matrix,
    mixing_score_matrix,
    mixing_final_matrix,
    alignment_expand_matrix,
    alignment_shrink_matrix,
    couple_expand_matrix,
    couple_shrink_matrix,
):
    send, own = call(first_kernel, [shape((TI, 64, 128)), shape((TOK, 256))], alignment_source)
    tokens = exchange(send, "ti", ORDER_TI)
    factors = call(factors_kernel, shape((TJ, 48, 128)), tokens, own, tensor_operand_matrix)
    factors = exchange(factors, "tj", ORDER_TJ)
    mid, logits = call(
        pair_kernel,
        [shape((COLS, TOK, 128)), shape((TJ, TOK, 128))],
        factors,
        couple_source,
        tensor_final_matrix,
        mixing_score_matrix.T,
        flops=2_000_000_000,
    )
    mid, tokens = lax.optimization_barrier((mid, tokens))
    logits = exchange(logits, "tj", ORDER_LOGITS)
    couple_result, values, gates = call(
        window_kernel,
        [shape((TOK, COLS, 128)), shape((2048, 256), BF16), shape((TOK, 1024))],
        mid,
        couple_expand_matrix,
        couple_shrink_matrix,
        tokens,
        mixing_content_matrix,
        own,
        mixing_switch_matrix,
        out_specs=[pl.BlockSpec(memory_space=pl.ANY), None, None],
        scratch=[pltpu.VMEM((TOK, COLS, 128), F32), pltpu.SemaphoreType.DMA(())],
        flops=2_000_000_000,
    )
    alignment_result = call(
        last_kernel,
        shape((ROWS, TOK, 64)),
        logits,
        values,
        gates,
        mixing_final_matrix.T,
        alignment_source,
        alignment_expand_matrix,
        alignment_shrink_matrix.T,
        flops=500_000_000,
    )
    return (alignment_result, couple_result)


def solution(mesh):
    rows, pairs = P("tj", "ti", None), P("ti", "tj", None)
    return jax.shard_map(
        shards,
        mesh=mesh,
        in_specs=(rows, pairs) + (P(),) * 10,
        out_specs=(rows, pairs),
        check_vma=False,
    )
```
